32 devices in a mesh: seq: 4 (over y, x), fsdp: 8 (over z, core).
Axes of the slice: x: 2, y: 2, z: 4, core: 2. Of those that a mesh axis runs over, the one named last changes fastest.
Arguments:
- tokens: bfloat16 [16, 1536, 1536], P('fsdp', 'seq'), may hold values from -6 to 6
- lengths: int32 [16], P('fsdp'), may hold values from 384 to 1536, as said below
- norm_gain: bfloat16 [1536], P('fsdp'), may hold values from 0.099609375 to 1.8984375
- in_weight: bfloat16 [1536, 4608], P('fsdp'), may hold values from -0.15625 to 0.15625
- conv_weight: bfloat16 [3, 1536], P(None, 'fsdp'), may hold values from -3 to 3
- out_weight: bfloat16 [1536, 1536], P('fsdp'), may hold values from -0.15625 to 0.15625
- ffn_gain: bfloat16 [1536], P('fsdp'), may hold values from 0.099609375 to 1.8984375
- gate_weight: bfloat16 [1536, 6912], P('fsdp'), may hold values from -0.15625 to 0.15625
- up_weight: bfloat16 [1536, 6912], P('fsdp'), may hold values from -0.15625 to 0.15625
- down_weight: bfloat16 [6912, 1536], P('fsdp'), may hold values from -0.078125 to 0.078125
- cotangent: bfloat16 [16, 1536, 1536], P('fsdp', 'seq'), may hold values from -6 to 6
Outputs:
- output: bfloat16 [16, 1536, 1536], P('fsdp', 'seq')
- tokens_grad: float32 [16, 1536, 1536], P('fsdp', 'seq')
- norm_gain_grad: float32 [1536], P('fsdp')
- in_weight_grad: float32 [1536, 4608], P('fsdp')
- conv_weight_grad: float32 [3, 1536], P(None, 'fsdp')
- out_weight_grad: float32 [1536, 1536], P('fsdp')
- ffn_gain_grad: float32 [1536], P('fsdp')
- gate_weight_grad: float32 [1536, 6912], P('fsdp')
- up_weight_grad: float32 [1536, 6912], P('fsdp')
- down_weight_grad: float32 [6912, 1536], P('fsdp')
The draws below stay inside these ranges and needn't reach their ends.
Inputs may be any that keep to these rules, and one draw needn't show every extreme that they name: `lengths`: each sequence's valid positions come first; at least one sequence is full length.
All inputs are finite; a program needn't handle non-finite values.
Results may differ from the reference program's by a relative error of at most 0.018.
Values may be sent and summed in bfloat16 or wider, within the bound.
A program may use at most 384 MiB of HBM per device.

```python
import math
import jax
import jax.numpy as jnp
from jax import lax

D = 1536
FF = 6912
LENGTH = 1536
SEQS = 16


def draw_lengths(key, part):
    drawn = jax.random.randint(jax.random.fold_in(key, 11), (SEQS,), LENGTH // 4, LENGTH + 1)
    chosen = jax.random.randint(jax.random.fold_in(key, 12), (), 0, SEQS)
    return jnp.where(jnp.arange(SEQS) == chosen, LENGTH, drawn).astype(jnp.int32)


def block_scale(stream_key, extent, split, low, high):
    loudness = 1.0
    for dim, blocks in split:
        draws = jax.random.uniform(jax.random.fold_in(jax.random.fold_in(stream_key, 6), dim), (blocks,), jnp.float32, low / len(split), high / len(split))
        loudness = loudness * jnp.repeat(jnp.exp(draws), extent[dim] // blocks).reshape((-1,) + (1,) * (len(extent) - 1 - dim))
    return loudness


def gaussian(stream_key, dims, scale, limit, pieces=(), kind=jnp.bfloat16):
    gain = block_scale(stream_key, dims, pieces, -0.22, 0.18) if pieces else 1.0
    values = jax.random.normal(stream_key, dims, jnp.float32) * scale * gain
    return jnp.minimum(jnp.maximum(values, -limit), limit).astype(kind)


def setup_inputs(seed: int = 0) -> dict:
    splits = jax.random.split(jax.random.key(seed), 12)
    tokens = gaussian(splits[0], (SEQS, LENGTH, D), 1.0, 6.0, ((0, 8), (1, 4)))
    lengths = draw_lengths(jax.random.fold_in(splits[11], 71), 0)
    norm_gain = jnp.clip(1.0 + 0.18 * jax.random.normal(splits[2], (D,), jnp.float32), 0.099609375, 1.8984375).astype(jnp.bfloat16)
    in_weight = gaussian(splits[3], (D, 3 * D), D ** -0.5, 0.15625, ((0, 8),))
    conv_weight = gaussian(splits[4], (3, D), 0.6, 3.0, ((1, 8),))
    out_weight = gaussian(splits[5], (D, D), D ** -0.5, 0.15625, ((0, 8),))
    ffn_gain = jnp.clip(1.0 + 0.18 * jax.random.normal(splits[6], (D,), jnp.float32), 0.099609375, 1.8984375).astype(jnp.bfloat16)
    gate_weight = gaussian(splits[7], (D, FF), D ** -0.5, 0.15625, ((0, 8),))
    up_weight = gaussian(splits[8], (D, FF), D ** -0.5, 0.15625, ((0, 8),))
    down_weight = gaussian(splits[9], (FF, D), FF ** -0.5, 0.078125, ((0, 8),))
    cotangent = gaussian(splits[10], (SEQS, LENGTH, D), 1.0, 6.0, ((0, 8), (1, 4)))
    return {"tokens": tokens, "lengths": lengths, "norm_gain": norm_gain, "in_weight": in_weight, "conv_weight": conv_weight, "out_weight": out_weight, "ffn_gain": ffn_gain, "gate_weight": gate_weight, "up_weight": up_weight, "down_weight": down_weight, "cotangent": cotangent}


EPS = 1e-05

@jax.custom_vjp
def low(v):
    return lax.optimization_barrier(v.astype(jnp.bfloat16)).astype(jnp.float32)

@jax.custom_vjp
def low_back(v):
    return v

def low_keep(v):
    return (low(v), None)

def low_pass(kept, grad):
    return (grad,)

def back_keep(v):
    return (v, None)

def back_low(kept, grad):
    return (low(grad),)
low.defvjp(low_keep, low_pass)
low_back.defvjp(back_keep, back_low)

def product(left, right):
    return jnp.einsum('gtd,de->gte', left, right, precision=lax.Precision.HIGHEST)

def forward(token_part, length_part, norm_gain, in_weight, conv_weight, out_weight, ffn_gain, gate_weight, up_weight, down_weight):
    seq_len = token_part.shape[1]
    model_width = token_part.shape[2]
    positions = jnp.arange(seq_len, dtype=jnp.int32)
    valid_rows = (positions[None, :] < length_part[:, None]).astype(jnp.float32)[..., None]
    scale_one = lax.rsqrt(lax.optimization_barrier(jnp.mean(token_part * token_part, -1, keepdims=True)) + EPS)
    normed_one = low(token_part * scale_one * norm_gain)
    projected = low_back(product(normed_one, in_weight))
    in_gate = projected[..., :model_width]
    out_gate = projected[..., model_width:2 * model_width]
    values = projected[..., 2 * model_width:]
    mixed = in_gate * values
    padded = jnp.pad(mixed, ((0, 0), (2, 0), (0, 0)))
    conv_out = conv_weight[0] * padded[:, :seq_len] + conv_weight[1] * padded[:, 1:seq_len + 1] + conv_weight[2] * padded[:, 2:]
    gated = low(out_gate * conv_out)
    hidden_one = token_part + low_back(product(gated, out_weight))
    scale_two = lax.rsqrt(lax.optimization_barrier(jnp.mean(hidden_one * hidden_one, -1, keepdims=True)) + EPS)
    normed_two = low(hidden_one * scale_two * ffn_gain)
    gate_pre = low_back(product(normed_two, gate_weight))
    up_pre = low_back(product(normed_two, up_weight))
    activated = low(jax.nn.silu(gate_pre) * up_pre)
    hidden_two = hidden_one + low_back(product(activated, down_weight))
    return valid_rows * hidden_two

def reference(tokens, lengths, norm_gain, in_weight, conv_weight, out_weight, ffn_gain, gate_weight, up_weight, down_weight, cotangent):
    weights = tuple((item.astype(jnp.float32) for item in (norm_gain, in_weight, conv_weight, out_weight, ffn_gain, gate_weight, up_weight, down_weight)))
    group_size = math.gcd(SEQS, max(1, 4096 // LENGTH))
    group_count = SEQS // group_size
    token_groups = tokens.astype(jnp.float32).reshape(group_count, group_size, LENGTH, D)
    cot_groups = cotangent.astype(jnp.float32).reshape(group_count, group_size, LENGTH, D)
    length_groups = lengths.reshape(group_count, group_size).astype(jnp.int32)

    def one_group(totals, inputs):
        token_part, cot_part, length_part = inputs

        def apply(token_arg, *weight_args):
            return forward(token_arg, length_part, *weight_args)
        result, pullback = jax.vjp(apply, token_part, *weights)
        grads = pullback(cot_part)
        totals = tuple((left + right for left, right in zip(totals, grads[1:])))
        return (totals, (result.astype(jnp.bfloat16), grads[0]))
    zeros = tuple((jnp.zeros(item.shape, jnp.float32) for item in weights))
    totals, (outputs, token_grads) = lax.scan(one_group, zeros, (token_groups, cot_groups, length_groups))
    return (outputs.reshape(SEQS, LENGTH, D), token_grads.reshape(SEQS, LENGTH, D), totals[0], totals[1], totals[2], totals[3], totals[4], totals[5], totals[6], totals[7])
```

```python
import functools

import jax
import jax.numpy as jnp
from jax import lax
from jax.experimental import pallas as pl
from jax.experimental.pallas import tpu as pltpu
from jax.sharding import PartitionSpec as P

EPS = 1e-05
MESH = pl.DeviceIdType.MESH

DMA = pltpu.SemaphoreType.DMA
ANY = pl.BlockSpec(memory_space=pl.ANY)


def rem(t, n):
    return t % n if isinstance(t, int) else lax.rem(t, n)


def remote(src, dst, send, recv, to):
    return pltpu.make_async_remote_copy(src_ref=src, dst_ref=dst, send_sem=send, recv_sem=recv, device_id=to, device_id_type=MESH)


class Here:
    def __init__(self):
        s, f = lax.axis_index("seq"), lax.axis_index("fsdp")
        self.s, self.f = s, f
        self.z, self.c = f // 2, lax.rem(f, 2)
        self.s0, self.s1 = lax.rem(s, 2), s // 2
        self.mate = (s, f + 1 - 2 * self.c)
        self.beside = (s + 1 - 2 * self.s0, s + 2 - 4 * self.s1)

    def greet(self, along=False):
        barrier = pltpu.get_barrier_semaphore()
        peers = [self.mate] + [(b, self.f) for b in self.beside] + [(self.s, lax.rem(self.f + 2 * j, 8)) for j in (1, 2, 3)]
        for peer in peers:
            pl.semaphore_signal(barrier, inc=1, device_id=peer, device_id_type=MESH)
        count = len(peers)
        if along:
            before, after = self.s > 0, self.s < 3
            for there, step in ((before, -1), (after, 1)):

                @pl.when(there)
                def _(step=step):
                    pl.semaphore_signal(barrier, inc=1, device_id=(jnp.clip(self.s + step, 0, 3), self.f), device_id_type=MESH)

            count = count + jnp.where(before, 1, 0) + jnp.where(after, 1, 0)
        pl.semaphore_wait(barrier, count)


class Reducer:
    def __init__(self, here, paired, held, total, fresh, landing, sems, core_source, goal):
        self.here, self.paired = here, paired
        self.held, self.fresh, self.total, self.landing = held, fresh, total, landing
        (self.local, self.core_s, self.core_r, self.one_s, self.one_r, self.two_s, self.two_r) = sems[:7]
        (self.z_s, self.z_r, self.near_s, self.near_r, self.far_s, self.far_r) = sems[7:]
        self.core_source, self.goal = core_source, goal
        self.slots, self.chips = held.shape[0], held.shape[2]

    def mine(self, t):
        return self.held.at[rem(t, self.slots)]

    def to_core(self, t):
        return remote(self.core_source(t), self.landing[0].at[t], self.core_s.at[t], self.core_r.at[t], self.here.mate)

    def one(self, t, d):
        h = self.here
        src = self.mine(t).at[0, :, :, 1 - h.s0] if d == 0 else self.mine(t).at[1, :, 1 - h.s1]
        return remote(src, self.landing[1 + d].at[t], self.one_s.at[t, d], self.one_r.at[t, d], (h.beside[d], h.f))

    def two(self, t, d):
        h = self.here
        src = self.mine(t).at[1, :, h.s1, 1 - h.s0] if d == 0 else self.mine(t).at[0, :, 1 - h.s1, h.s0]
        return remote(src, self.landing[4 - d].at[t], self.two_s.at[t, d], self.two_r.at[t, d], (h.beside[d], h.f))

    def part(self, t, a):
        h = self.here
        if self.paired:
            return self.mine(t).at[:, a, h.s1, h.s0]
        return self.mine(t).at[a // 2, lax.rem(a, 2), h.s1, h.s0]

    def to_chip(self, t, j):
        h = self.here
        a = lax.rem(h.z + j, 4)
        slot = jnp.where(h.z < a, h.z, h.z - 1)
        return remote(self.part(t, a), self.landing[5].at[t, slot], self.z_s.at[t, j - 1], self.z_r.at[t, slot], (h.s, 2 * a + h.c))

    def from_chip(self, t, slot):
        h = self.here
        return remote(self.part(t, 0), self.landing[5].at[t, slot], self.z_s.at[t, 0], self.z_r.at[t, slot], h.mate)

    def keep(self, t):
        return pltpu.make_async_copy(self.total.at[rem(t, 2)], self.goal(t, self.here.s, None), self.local.at[8 + rem(t, 2)])

    def near(self, t, d):
        h = self.here
        return remote(self.total.at[rem(t, 2)], self.goal(t, h.s, None), self.near_s.at[t, d], self.near_r.at[t, d], (h.beside[d], h.f))

    def far(self, t, d):
        h = self.here
        ref = self.goal(t, h.beside[1 - d], d)
        return remote(ref, ref, self.far_s.at[t, d], self.far_r.at[t, d], (h.beside[d], h.f))

    def pending(self, src, dst, which):
        return pltpu.make_async_copy(src, dst, self.local.at[which])

    def bring(self, src, dst, which):
        self.pending(src, dst, which).start()

    def stage0(self, t):
        self.to_core(t).start()

    def fetch1(self, t):
        self.to_core(t).wait_recv()
        self.bring(self.landing[0].at[t], self.fresh[0], 0)

    def stage1(self, t):
        fresh, me = self.fresh[0], self.mine(t)
        self.pending(self.landing[0].at[t], fresh, 0).wait()

        @pl.loop(0, 2 * self.chips)
        def _(i):
            at = (i // self.chips, lax.rem(i, self.chips))
            me[at] = me[at] + fresh[at]

        self.one(t, 0).start()
        self.one(t, 1).start()

    def fetch2(self, t):
        for d in (0, 1):
            self.one(t, d).wait_recv()
            self.bring(self.landing[1 + d].at[t], self.fresh[1].at[d], 1 + d)

    def stage2(self, t):
        h, fresh, me = self.here, self.fresh[1], self.mine(t)
        for d in (0, 1):
            self.pending(self.landing[1 + d].at[t], fresh.at[d], 1 + d).wait()

        @pl.loop(0, self.chips)
        def _(a):
            for b in (0, 1):
                me[0, a, b, h.s0] = me[0, a, b, h.s0] + fresh[0, a, b]
                me[1, a, h.s1, b] = me[1, a, h.s1, b] + fresh[1, a, b]

        self.two(t, 1).start()
        self.two(t, 0).start()

    def fetch3(self, t):
        for d in (1, 0):
            self.two(t, d).wait_recv()
            self.bring(self.landing[4 - d].at[t], self.fresh[2].at[1 - d], 4 - d)

    def stage3(self, t):
        h, fresh, me = self.here, self.fresh[2], self.mine(t)
        for d in (1, 0):
            self.pending(self.landing[4 - d].at[t], fresh.at[1 - d], 4 - d).wait()

        @pl.loop(0, self.chips)
        def _(a):
            me[0, a, h.s1, h.s0] = me[0, a, h.s1, h.s0] + fresh[0, a]
            me[1, a, h.s1, h.s0] = me[1, a, h.s1, h.s0] + fresh[1, a]

        for j in (1, 2, 3):
            self.to_chip(t, j).start()

    def fetch4(self, t):
        for slot in range(3):
            self.from_chip(t, slot).wait_recv()
            self.bring(self.landing[5].at[t, slot], self.fresh[3].at[slot], 5 + slot)

    def stage4(self, t):
        h, fresh = self.here, self.fresh[3]
        for slot in range(3):
            self.pending(self.landing[5].at[t, slot], fresh.at[slot], 5 + slot).wait()
        acc = self.part(t, h.z)[...].astype(jnp.float32)
        for slot in range(3):
            acc += fresh[slot].astype(jnp.float32)
        self.total[rem(t, 2)] = acc.astype(jnp.bfloat16)
        self.near(t, 0).start()
        self.near(t, 1).start()
        self.keep(t).start()
        for d in (0, 1):
            self.one(t, d).wait_send()
            self.two(t, d).wait_send()
        for j in (1, 2, 3):
            self.to_chip(t, j).wait_send()

    def near_in(self, t, d):
        h = self.here
        ref = self.goal(t, h.beside[d], None)
        return remote(ref, ref, self.near_s.at[t, d], self.near_r.at[t, d], (h.beside[d], h.f))

    def far_in(self, t, d):
        h = self.here
        ref = self.goal(t, 3 - h.s, d)
        return remote(ref, ref, self.far_s.at[t, d], self.far_r.at[t, d], (h.beside[d], h.f))

    def stage5(self, t):
        self.near_in(t, 1).wait_recv()
        self.far(t, 0).start()
        self.near_in(t, 0).wait_recv()
        self.far(t, 1).start()
        self.near(t, 0).wait_send()
        self.near(t, 1).wait_send()
        self.keep(t).wait()

    def stage6(self, t):
        for d in (0, 1):
            self.far_in(t, d).wait_recv()
            self.far(t, d).wait_send()


def landing_shapes(n, paired, rows, width):
    chips = 4 if paired else 2
    lead = (2,) if paired else ()
    shapes = [(n, 2, chips, 2, 2, rows, width)] + [(n, chips, 2, rows, width)] * 2 + [(n, chips, rows, width)] * 2 + [(n, 3) + lead + (rows, width)]
    return [jax.ShapeDtypeStruct(shape, jnp.bfloat16) for shape in shapes]


def scratch_shapes(slots, paired, rows, width):
    chips = 4 if paired else 2
    lead = (2,) if paired else ()
    shapes = [(slots, 2, chips, 2, 2, rows, width), (2,) + lead + (rows, width)]
    shapes += [(2, chips, 2, 2, rows, width), (2, chips, 2, rows, width), (2, chips, rows, width), (3,) + lead + (rows, width)]
    return [pltpu.VMEM(shape, jnp.bfloat16) for shape in shapes]


def sem_shapes(n):
    return [DMA((10,)), DMA((n,)), DMA((n,))] + [DMA((n, 2))] * 4 + [DMA((n, 3))] * 2 + [DMA((n, 2))] * 4


def halves(rows):
    half = (rows // 2 + 7) // 8 * 8
    return {None: pl.ds(0, rows), 0: pl.ds(0, half), 1: pl.ds(half, rows - half)}


TILE = 256
SUBS = 3
SLOTS = 5


def dot_nn(a, b):
    return lax.dot_general(a, b, (((1,), (0,)), ((), ())), preferred_element_type=jnp.float32)


def dot_nt(a, b):
    return lax.dot_general(a, b, (((1,), (1,)), ((), ())), preferred_element_type=jnp.float32)


def dot_tn(a, b):
    return lax.dot_general(a, b, (((0,), (0,)), ((), ())), preferred_element_type=jnp.float32)


def ffn_kernel(tiles, n2, mine_t, mate_t, down_in, keep, w_gate, w_up, w_down, hidden, *refs):
    output, back, grad_down, shards = refs[:4]
    landing = refs[4:10]
    act, gate_back, up_back, outgoing, held, total = refs[10:16]
    fresh, sems = refs[16:20], refs[20:33]
    y, start_sem = refs[33:]
    hidden_in = pltpu.make_async_copy(hidden, y, start_sem)
    i = pl.program_id(0)
    chunks = tiles // SUBS
    here = Here()
    width = TILE * SUBS
    rows = shards.shape[2]
    spans = halves(rows)

    def goal(t, quarter, part):
        return shards.at[:, quarter, spans[part], pl.ds(pl.multiple_of(t * width, width), width)]

    red = Reducer(here, True, held, total, fresh, landing, sems, lambda t: outgoing.at[lax.rem(t, 2)], goal)

    def hook(offset, *stages):
        past = i - offset
        t = past // SUBS

        @pl.when((past >= 0) & (lax.rem(past, SUBS) == 0) & (t < chunks))
        def _():
            for stage in stages:
                stage(t)

    @pl.when(i == 0)
    def _():
        here.greet()
        hidden_in.start()
        back[...] = jnp.zeros_like(back)

    @pl.when(i < tiles)
    def _():
        g = dot_nn(n2[...], w_gate[...])
        u = dot_nn(n2[...], w_up[...])
        a = dot_nt(down_in[...], w_down[...])
        sig = jax.nn.sigmoid(g)
        silu = g * sig
        act[...] = (silu * u).astype(jnp.bfloat16)
        gate_back[...] = (a * u * (sig * (1.0 + g * (1.0 - sig)))).astype(jnp.bfloat16)
        up_back[...] = (a * silu).astype(jnp.bfloat16)

    hook(7, red.stage2)
    hook(13, red.fetch4)

    @pl.when(i == 0)
    def _():
        hidden_in.wait()

    @pl.when(i == tiles)
    def _():
        output[...] = (y[...] * keep[...]).astype(jnp.bfloat16)

    @pl.when(i < tiles)
    def _():
        @pl.loop(0, 3)
        def _(j):
            at = pl.ds(pl.multiple_of(j * 512, 512), 512)
            y[:, at] += dot_nn(act[...], w_down[:, at])
            back[:, at] += dot_nt(gate_back[...], w_gate[at, :]) + dot_nt(up_back[...], w_up[at, :])
            grad_down[:, at] = dot_tn(act[...], down_in[:, at]).astype(jnp.bfloat16)

    hook(3, red.fetch1)
    hook(10, red.fetch3)
    chunk, sub = i // SUBS, lax.rem(i, SUBS)

    @pl.when((sub == 0) & (chunk >= 2) & (chunk < chunks + 2))
    def _():
        red.to_core(chunk - 2).wait_send()

    @pl.when(i < tiles)
    def _():
        at = pl.ds(pl.multiple_of(sub * TILE, TILE), TILE)
        out, me = outgoing.at[lax.rem(chunk, 2)], red.mine(chunk)
        shape = (4, 2, 2, rows, TILE)
        for m, grad in ((0, gate_back), (1, up_back)):
            out[m, :, :, :, :, at] = dot_nn(mate_t[...], grad[...]).astype(jnp.bfloat16).reshape(shape)
            me[m, :, :, :, :, at] = dot_nn(mine_t[...], grad[...]).astype(jnp.bfloat16).reshape(shape)

    hook(3, red.stage1)
    hook(6, red.fetch2)
    hook(10, red.stage3)
    hook(13, red.stage4)
    hook(16, red.stage5)
    hook(19, red.stage6)

    @pl.when((sub == SUBS - 1) & (chunk < chunks))
    def _():
        red.stage0(chunk)


def ffn(n2, mine_t, mate_t, down_in, keep, w_gate, w_up, w_down, hidden_one, cid):
    m, d = n2.shape
    hidden = w_gate.shape[1]
    tiles = hidden // TILE
    chunks, width = tiles // SUBS, TILE * SUBS
    rows = d // 32
    one = lambda *shape: pl.BlockSpec(shape, lambda i: (0, 0), pipeline_mode=pl.Buffered(1))
    across = pl.BlockSpec((d, TILE), lambda i: (0, jnp.minimum(i, tiles - 1)))
    down = pl.BlockSpec((TILE, d), lambda i: (jnp.minimum(i, tiles - 1), 0))
    out_shape = [jax.ShapeDtypeStruct((m, d), jnp.bfloat16), jax.ShapeDtypeStruct((m, d), jnp.float32)] + [jax.ShapeDtypeStruct((hidden, d), jnp.bfloat16), jax.ShapeDtypeStruct((2, 4, rows, hidden), jnp.bfloat16)]
    out_shape += landing_shapes(chunks, True, rows, width)
    res = pl.pallas_call(
        functools.partial(ffn_kernel, tiles),
        grid=(tiles + 17,),
        out_shape=out_shape,
        in_specs=[one(m, d), one(d // 2, m), one(d // 2, m), one(m, d), one(m, 1), across, across, down, ANY],
        out_specs=[one(m, d), one(m, d), down, ANY] + [ANY] * 6,
        scratch_shapes=[pltpu.VMEM((m, TILE), jnp.bfloat16)] * 3
        + [pltpu.VMEM((2, 2, 4, 2, 2, rows, width), jnp.bfloat16)]
        + scratch_shapes(SLOTS, True, rows, width)
        + sem_shapes(chunks)
        + [pltpu.VMEM((m, d), jnp.float32), DMA],
        compiler_params=pltpu.CompilerParams(collective_id=cid, has_side_effects=True, vmem_limit_bytes=61 << 20),
        name="ffn",
    )(n2, mine_t, mate_t, down_in, keep, w_gate, w_up, w_down, hidden_one)
    return res[:4]


def front_kernel(count, *refs):
    shards, small, tokens = refs[:count], refs[count], refs[count + 1]
    at = count + 2
    fulls = refs[at : at + count]
    normed_one, projected, edges, vectors, hidden_out, normed_two, mine_t, mate_t = refs[at + count : at + count + 8]
    at += count + 8
    (local_sem, core_send, core_recv, z_send, z_recv, near_send, near_recv, far_send, far_recv, small_send, small_recv) = refs[at : at + 11]
    at += 11
    staged = refs[at : at + count]
    smalls, weights, part, mixed, gated, hidden, turned, work_sem, edge_s, edge_r = refs[at + count :]
    s, f = lax.axis_index("seq"), lax.axis_index("fsdp")
    z, c = f // 2, lax.rem(f, 2)
    mate = f + 1 - 2 * c
    beside = (s + 1 - 2 * lax.rem(s, 2), s + 2 - 4 * (s // 2))
    last = 3
    flip = z >= 2
    zf = jnp.where(flip, last - z, z)

    def source(j):
        a = jnp.where(j < zf, j, j + 1)
        return jnp.where(flip, last - a, a)

    def slot(at, a):
        turned = at >= 2
        at = jnp.where(turned, last - at, at)
        a = jnp.where(turned, last - a, a)
        return jnp.where(a < at, a, a - 1)

    barrier = pltpu.get_barrier_semaphore()
    for k in range(1, 8):
        pl.semaphore_signal(barrier, inc=1, device_id=(s, lax.rem(f + k, 8)), device_id_type=MESH)
    for b in beside:
        pl.semaphore_signal(barrier, inc=1, device_id=(b, f), device_id_type=MESH)
    before, after = s > 0, s < 3
    for there, step in ((before, -1), (after, 1)):

        @pl.when(there)
        def _(step=step):
            pl.semaphore_signal(barrier, inc=1, device_id=(jnp.clip(s + step, 0, 3), f), device_id_type=MESH)

    pl.semaphore_wait(barrier, 9 + jnp.where(before, 1, 0) + jnp.where(after, 1, 0))

    def remote(src, dst, send, recv, to):
        return pltpu.make_async_remote_copy(src_ref=src, dst_ref=dst, send_sem=send, recv_sem=recv, device_id=to, device_id_type=MESH)

    def rows(m, shard_index, quarter=None, part=None):
        r = shards[m].shape[0]
        start, size = shard_index * r, r
        if quarter is not None:
            size = r // 4
            start = start + quarter * size
            half = (size // 2 + 7) // 8 * 8
            if part == 0:
                size = half
            elif part == 1:
                start, size = start + half, size - half
        return pl.ds(pl.multiple_of(start, 8), size)

    def place(m, *where):
        return fulls[m].at[rows(m, *where)]

    def load(m):
        return pltpu.make_async_copy(shards[m], staged[m], local_sem.at[m])

    def keep(m):
        return pltpu.make_async_copy(staged[m], place(m, f), local_sem.at[m])

    def own_core(m):
        return remote(shards[m], place(m, f), core_send.at[m, 3], core_recv.at[m, 3], (s, mate))

    def z_own(m, up):
        to = z + 1 if up else z - 1
        return remote(shards[m].at[rows(m, 0, s)], place(m, f, s), z_send.at[m, 3 + up], z_recv.at[m, slot(to, z)], (s, 2 * to + c))

    def z_on(m, j):
        a = source(j)
        to = jnp.where(a < z, z + 1, z - 1)
        at = place(m, 2 * a + c, s)
        to_safe = jnp.clip(to, 0, last)
        return remote(at, at, z_send.at[m, j], z_recv.at[m, jnp.clip(slot(to_safe, a), 0, 2)], (s, 2 * to_safe + c))

    def z_in(m, j):
        at = place(m, 2 * source(j) + c, s)
        return remote(at, at, z_send.at[m, j], z_recv.at[m, j], (s, f))

    def goes_on(j):
        a = source(j)
        return jnp.where(a < z, z < last, z > 0)

    def near(m, j, d):
        at = place(m, 2 * source(j) + c, s)
        return remote(at, at, near_send.at[m, j, d], near_recv.at[m, j, d], (beside[d], f))

    def far(m, j, d):
        at = place(m, 2 * source(j) + c, beside[1 - d], d)
        return remote(at, at, far_send.at[m, j, d], far_recv.at[m, j, d], (beside[d], f))

    def core(m, j):
        at = place(m, 2 * source(j) + c)
        return remote(at, at, core_send.at[m, j], core_recv.at[m, j], (s, mate))

    def begin(m):
        @pl.when(z < last)
        def _():
            z_own(m, 1).start()
        @pl.when(z > 0)
        def _():
            z_own(m, 0).start()
        load(m).start()
        own_core(m).start()

    def spread(m, j):
        z_in(m, j).wait_recv()
        @pl.when(goes_on(j))
        def _():
            z_on(m, j).start()
        near(m, j, 0).start()
        near(m, j, 1).start()
        if j == 0:
            load(m).wait()
            keep(m).start()

    def diagonal(m, j):
        near(m, j, 1).wait_recv()
        far(m, j, 0).start()
        near(m, j, 0).wait_recv()
        far(m, j, 1).start()

    def share(m, j):
        far(m, j, 0).wait_recv()
        far(m, j, 1).wait_recv()
        core(m, j).start()

    def finish(m, j):
        if j == 0:
            keep(m).wait()
            own_core(m).wait()
            @pl.when(z < last)
            def _():
                z_own(m, 1).wait_send()
            @pl.when(z > 0)
            def _():
                z_own(m, 0).wait_send()
        @pl.when(goes_on(j))
        def _():
            z_on(m, j).wait_send()
        for d in (0, 1):
            near(m, j, d).wait_send()
            far(m, j, d).wait_send()
        core(m, j).wait()

    def small_copy(k):
        return remote(small, smalls.at[f], small_send.at[k - 1], small_recv.at[k - 1], (s, lax.rem(f + k, 8)))

    depth = tokens.shape[1]
    blocks = depth // 256
    seqs, length = mixed.shape[0], mixed.shape[1] - 8
    gain_one, taps, gain_two = 0, 1, 4

    def small_step():
        vectors[...] = jnp.zeros(vectors.shape, jnp.float32)
        for k in range(8):
            if k:
                small_copy(k).wait()
            start = lax.rem(f + 8 - k, 8) * (depth // 8) // 128 * 128
            at = pl.ds(pl.multiple_of(start, 128), small.shape[1])
            vectors[:, at] = vectors[:, at] + (smalls[k - 1] if k else small[...])

    def norm_one_step():
        @pl.loop(0, tokens.shape[0] // 64)
        def _(r):
            at = pl.ds(pl.multiple_of(r * 64, 64), 64)
            token_rows = tokens[at, :].astype(jnp.float32)
            scale = lax.rsqrt(jnp.mean(token_rows * token_rows, -1, keepdims=True) + EPS)
            normed_one[at, :] = (token_rows * scale * vectors[gain_one : gain_one + 1, :]).astype(jnp.bfloat16)

    def weight_in(j):
        slot = j % 2
        return [
            pltpu.make_async_copy(fulls[1].at[:, pl.ds(g * depth + j * 256, 256)], weights.at[slot, g], work_sem.at[3 * slot + g])
            for g in range(3)
        ]

    def part_out(j):
        slot = j % 2
        return [
            pltpu.make_async_copy(part.at[slot, g], projected.at[:, pl.ds(g * depth + j * 256, 256)], work_sem.at[6 + 3 * slot + g])
            for g in range(3)
        ]

    def start_all(copies):
        for copy in copies:
            copy.start()

    def wait_all(copies):
        for copy in copies:
            copy.wait()

    def project_step(j):
        slot, at = j % 2, slice(j * 256, (j + 1) * 256)
        if j == 0:
            start_all(weight_in(0))
        wait_all(weight_in(j))
        if j + 1 < blocks:
            start_all(weight_in(j + 1))
        if j >= 2:
            wait_all(part_out(j - 2))
        for g in range(3):
            part[slot, g] = dot_nn(normed_one[...], weights[slot, g]).astype(jnp.bfloat16)
        start_all(part_out(j))
        gated[:, at] = part[slot, 1]
        for q in range(seqs):
            span = slice(q * length, (q + 1) * length)
            mixed[q, 8:, at] = part[slot, 0, span, :].astype(jnp.float32) * part[slot, 2, span, :].astype(jnp.float32)

    def edge_copy():
        return remote(mixed.at[:, length : length + 8], mixed.at[:, 0:8], edge_s, edge_r, (jnp.minimum(s + 1, 3), f))

    def edge_start():
        wait_all(part_out(blocks - 2))
        wait_all(part_out(blocks - 1))

        @pl.when(jnp.logical_not(before))
        def _():
            mixed[:, 0:8, :] = jnp.zeros((seqs, 8, depth), jnp.float32)

        @pl.when(after)
        def _():
            edge_copy().start()

        start_all([out_in(0)])

    def edge_wait():
        @pl.when(after)
        def _():
            edge_copy().wait_send()

        @pl.when(before)
        def _():
            edge_copy().wait_recv()

        edges[...] = mixed[:, 0:8, :]

    def conv_step(j):
        at = slice(j * 256, (j + 1) * 256)
        for q in range(seqs):
            span = slice(q * length, (q + 1) * length)
            conv = sum(vectors[taps + k : taps + k + 1, at] * mixed[q, 6 + k : 6 + k + length, at] for k in range(3))
            gated[span, at] = (gated[span, at].astype(jnp.float32) * conv).astype(jnp.bfloat16)

    def out_in(j):
        return pltpu.make_async_copy(fulls[0].at[:, pl.ds(j * 256, 256)], weights.at[j % 2, 0], work_sem.at[3 * (j % 2)])

    def out_step(j):
        at = slice(j * 256, (j + 1) * 256)
        out_in(j).wait()
        if j + 1 < blocks:
            out_in(j + 1).start()
        hidden[:, at] = tokens[:, at].astype(jnp.float32) + dot_nn(gated[...], weights[j % 2, 0])

    hidden_copy = pltpu.make_async_copy(hidden, hidden_out, work_sem.at[12])

    def norm_two_step():
        hidden_copy.start()

        @pl.loop(0, tokens.shape[0] // 64)
        def _(r):
            at = pl.ds(pl.multiple_of(r * 64, 64), 64)
            rows_two = hidden[at, :]
            scale = lax.rsqrt(jnp.mean(rows_two * rows_two, -1, keepdims=True) + EPS)
            normed_two[at, :] = (rows_two * scale * vectors[gain_two : gain_two + 1, :]).astype(jnp.bfloat16)

    shard = depth // 8

    def turned_out():
        copies = []
        for chip in range(4):
            for goal, core_of, sem in ((mine_t, c, 0), (mate_t, 1 - c, 4)):
                start = pl.multiple_of((2 * chip + core_of) * shard, 16)
                copies.append(pltpu.make_async_copy(turned.at[pl.ds(start, shard)], goal.at[pl.ds(chip * shard, shard)], work_sem.at[sem + chip]))
        return copies

    def turn_step():
        @pl.loop(0, blocks)
        def _(r):
            at = pl.ds(pl.multiple_of(r * 256, 256), 256)
            turned[at, :] = normed_two[:, at].T

        start_all(turned_out())

    def each(step, *js):
        return [functools.partial(step, j) for j in js]

    work = {3: [small_step], 5: [norm_one_step]}
    first = 3 * 2 + 5
    work[first] = each(project_step, 0, 1)
    work[first + 1] = each(project_step, 2, 3)
    work[first + 2] = each(project_step, 4, 5) + [edge_start]
    work[first + 3] = [edge_wait] + each(conv_step, *range(blocks))
    work[first + 4] = each(out_step, *range(blocks))
    work[first + 5] = [norm_two_step, turn_step]

    def small_copy(k):
        return remote(small, smalls.at[k - 1], small_send.at[k - 1], small_recv.at[k - 1], (s, lax.rem(f + k, 8)))

    begin(0)
    for k in range(1, 8):
        small_copy(k).start()
    stages = (spread, diagonal, share, finish)
    lag = (0, 1, 3, 5)
    for step in range(3 * count + lag[-1]):
        for stage, by in zip(stages, lag):
            if 0 <= step - by < 3 * count:
                m, j = divmod(step - by, 3)
                stage(m, j)
                if stage is spread and j == 1 and m + 1 < count:
                    begin(m + 1)
        for piece in work.get(step, []):
            piece()
    hidden_copy.wait()
    wait_all(turned_out())


def front(shards, small, tokens, cid):
    count = len(shards)
    anyspec = pl.BlockSpec(memory_space=pl.ANY)
    whole = pl.BlockSpec(memory_space=pltpu.VMEM)
    vmem = pltpu.VMEM
    dma = pltpu.SemaphoreType.DMA
    sds = jax.ShapeDtypeStruct
    rows, depth = tokens.shape
    half, full = jnp.bfloat16, jnp.float32
    outs = [sds((8 * a.shape[0], a.shape[1]), a.dtype) for a in shards]
    outs += [sds((rows, depth), half), sds((rows, 3 * depth), half), sds((2, 8, depth), full), sds((8, depth), full), sds((rows, depth), full)]
    outs += [sds((rows, depth), half), sds((depth // 2, rows), half), sds((depth // 2, rows), half)]
    return pl.pallas_call(
        functools.partial(front_kernel, count),
        out_shape=outs,
        in_specs=[anyspec] * count + [whole] * 2,
        out_specs=[anyspec] * count + [whole, anyspec, whole, whole, anyspec, whole, anyspec, anyspec],
        scratch_shapes=[dma((count,)), dma((count, 4)), dma((count, 4)), dma((count, 5)), dma((count, 3))]
        + [dma((count, 3, 2))] * 4
        + [dma((7,)), dma((7,))]
        + [vmem(a.shape, a.dtype) for a in shards]
        + [vmem((7,) + small.shape, full), vmem((2, 3, depth, 256), half), vmem((2, 3, rows, 256), half), vmem((2, rows // 2 + 8, depth), full)]
        + [vmem((rows, depth), half), vmem((rows, depth), full), vmem((depth, rows), half), dma((13,)), dma, dma],
        compiler_params=pltpu.CompilerParams(collective_id=cid, has_side_effects=True, vmem_limit_bytes=58 << 20),
        name="front",
    )(*shards, small, tokens)


def mix_kernel(plan, kinds, *refs):
    arrays, n = max(p[1] for p in plan) + 1, len(kinds)
    grads = list(refs[: arrays - 2])
    normed, down_in, tokens, edges, taps, gain_one, gain_two, w_in, w_out, projected, back, hidden = refs[arrays - 2 : arrays + 10]
    at = arrays + 10
    outs, small_out, tokens_grad, grad_out, grad_in = refs[at : at + arrays], *refs[at + arrays : at + arrays + 4]
    at += arrays + 4
    grads += [grad_out, grad_in]
    landing = [refs[at + 6 * k : at + 6 * k + 6] for k in range(n)]
    at += 6 * n
    scratch = [refs[at + 6 * k : at + 6 * k + 6] for k in range(n)]
    at += 6 * n
    sems = [refs[at + 13 * k : at + 13 * k + 13] for k in range(n)]
    at += 13 * n
    own_sem, small_own, small_land, small_s, small_r, normed_t, block, weights, normed_grad, residual, work_sem = refs[at : at + 11]
    proj_back, out_back, conv_grad, part, mixed, rows_out, edge_s, edge_r = refs[at + 11 :]
    here = Here()
    here.greet(True)

    def columns(k, t):
        return [p for p in plan if p[0] == k][t]

    reducers = []
    for k, (rows, width) in enumerate(kinds):
        spans = halves(rows)

        def source(t, core, k=k, width=width):
            _, array, column = columns(k, t)
            if array >= arrays - 2:
                whole = grads[array].shape
                return grads[array].reshape(2, 2, 2, 2, 2, whole[0] // 32, whole[1]).at[:, :, core, :, :, :, pl.ds(column, width)]
            return grads[array].at[:, :, core, :, :, :, pl.ds(column, width)]

        def goal(t, quarter, part, k=k, width=width, spans=spans):
            _, array, column = columns(k, t)
            return outs[array].at[quarter, spans[part], pl.ds(column, width)]

        held, total, *fresh = scratch[k]
        red = Reducer(here, False, held, total, fresh, landing[k], sems[k], lambda t, source=source: source(t, 1 - here.c), goal)
        red.own = lambda t, k=k, source=source, red=red: pltpu.make_async_copy(source(t, here.c), red.mine(t), own_sem.at[k])
        reducers.append(red)

    def stage1(red, t):
        red.own(t).start()
        red.fetch1(t)
        red.own(t).wait()
        red.stage1(t)

    def both(name):
        def run(red, t):
            getattr(red, "fetch" + name)(t)
            getattr(red, "stage" + name)(t)

        return run

    hops = [here.mate, (here.beside[0], here.f), (here.beside[1], here.f)]

    def small_hop(j):
        return remote(small_own.at[j], small_land.at[j], small_s.at[j], small_r.at[j], hops[j])

    def small_chip(j):
        a = lax.rem(here.z + j, 4)
        return remote(small_own.at[3], small_land.at[2 + j], small_s.at[2 + j], small_r.at[2 + j], (here.s, 2 * a + here.c))

    def small_step(j):
        if j < 3:
            small_hop(j).wait()
            small_own[j + 1] = small_own[j] + small_land[j]
            if j < 2:
                small_hop(j + 1).start()
            else:
                for i in (1, 2, 3):
                    small_chip(i).start()
        else:
            for i in (1, 2, 3):
                small_chip(i).wait()
            small_out[...] = small_own[3] + small_land[3] + small_land[4] + small_land[5]

    width, depth = proj_back.shape[1], normed.shape[1]
    chunk = block.shape[1]

    def block_out(j):
        return pltpu.make_async_copy(block, grad_in.at[:, pl.ds(j * chunk, chunk)], work_sem.at[0])

    def turn():
        @pl.loop(0, depth // 256)
        def _(r):
            at = pl.ds(pl.multiple_of(r * 256, 256), 256)
            normed_t[at, :] = normed[:, at].T

    def grad_in_step(j):
        if j == 0:
            turn()
        else:
            block_out(j - 1).wait()

        @pl.loop(0, depth // 256)
        def _(r):
            at = pl.ds(pl.multiple_of(r * 256, 256), 256)
            block[at, :] = dot_nn(normed_t[at, :], proj_back[:, j * chunk : (j + 1) * chunk]).astype(jnp.bfloat16)

        block_out(j).start()

    blocks = depth // 256

    def weight_in(j):
        return pltpu.make_async_copy(w_in.at[pl.ds(j * 256, 256)], weights.at[j % 2], work_sem.at[1 + j % 2])

    hidden_in = pltpu.make_async_copy(hidden, residual, work_sem.at[3])
    back_in = pltpu.make_async_copy(back, normed_grad, work_sem.at[4])
    result_out = pltpu.make_async_copy(normed_grad, tokens_grad, work_sem.at[3])

    def back_step(j):
        weight_in(j).wait()
        if j + 1 < blocks:
            weight_in(j + 1).start()
        normed_grad[:, j * 256 : (j + 1) * 256] = dot_nt(proj_back[...], weights[j % 2])

    def norm_step():
        @pl.loop(0, normed.shape[0] // 64)
        def _(r):
            at = pl.ds(pl.multiple_of(r * 64, 64), 64)
            token_rows = tokens[at, :].astype(jnp.float32)
            scale = lax.rsqrt(jnp.mean(token_rows * token_rows, -1, keepdims=True) + EPS)
            unit = token_rows * scale
            grad = normed_grad[at, :]
            small_own[0, 0:1, :] += jnp.sum(grad * unit, 0, keepdims=True)
            inner = grad * gain_one[...]
            normed_grad[at, :] = residual[at, :] + scale * (inner - unit * jnp.mean(inner * unit, -1, keepdims=True))

        result_out.start()
        small_hop(0).start()

    def norm_two_step():
        hidden_in.wait()
        back_in.wait()
        small_own[0] = jnp.zeros(small_own.shape[1:], jnp.float32)

        @pl.loop(0, normed.shape[0] // 64)
        def _(r):
            at = pl.ds(pl.multiple_of(r * 64, 64), 64)
            rows_two = residual[at, :]
            scale = lax.rsqrt(jnp.mean(rows_two * rows_two, -1, keepdims=True) + EPS)
            unit = rows_two * scale
            grad = normed_grad[at, :]
            small_own[0, 4:5, :] += jnp.sum(grad * unit, 0, keepdims=True)
            inner = grad * gain_two[...]
            total = down_in[at, :].astype(jnp.float32) + scale * (inner - unit * jnp.mean(inner * unit, -1, keepdims=True))
            residual[at, :] = total
            out_back[at, :] = total.astype(jnp.bfloat16)

    seqs, length = mixed.shape[0], mixed.shape[1] - 8

    def part_in(j):
        slot = j % 2
        return [
            pltpu.make_async_copy(projected.at[:, pl.ds(g * depth + (j % blocks) * 256, 256)], part.at[slot, g], work_sem.at[5 + 3 * slot + g])
            for g in range(3)
        ]

    def out_weight_in(j):
        return pltpu.make_async_copy(w_out.at[pl.ds(j * 256, 256)], weights.at[j % 2, :, 0:depth], work_sem.at[11 + j % 2])

    def rows_out_copy(j):
        return pltpu.make_async_copy(rows_out, grad_out.at[pl.ds(j * 256, 256)], work_sem.at[0])

    def start_block(j):
        if j < 2 * blocks:
            for copy in part_in(j):
                copy.start()
        if j < blocks:
            out_weight_in(j).start()

    def conv_step(j):
        for copy in part_in(j):
            copy.wait()
        out_weight_in(j).wait()
        start_block(j + 1)
        slot, at = j % 2, slice(j * 256, (j + 1) * 256)
        gated_grad = dot_nt(out_back[...], weights[slot, :, 0:depth])
        if j:
            rows_out_copy(j - 1).wait()
        for q in range(seqs):
            span = slice(q * length, (q + 1) * length)
            out_gate = part[slot, 1, span, :].astype(jnp.float32)
            mixed[q, 0:8, :] = edges[q, :, at]
            mixed[q, 8:, :] = part[slot, 0, span, :].astype(jnp.float32) * part[slot, 2, span, :].astype(jnp.float32)
            shifted = [mixed[q, 6 + k : 6 + k + length, :] for k in range(3)]
            conv = sum(taps[k : k + 1, at] * shifted[k] for k in range(3))
            grad = gated_grad[span, :]
            proj_back[span, depth + j * 256 : depth + (j + 1) * 256] = (grad * conv).astype(jnp.bfloat16)
            part[slot, 1, span, :] = (out_gate * conv).astype(jnp.bfloat16)
            grad = grad * out_gate
            conv_grad[q, 0:length, at] = grad
            for k in range(3):
                small_own[0, 1 + k : 2 + k, at] += jnp.sum(grad * shifted[k], 0, keepdims=True)
        rows_out[...] = dot_tn(part[slot, 1], out_back[...]).astype(jnp.bfloat16)
        rows_out_copy(j).start()

    last = here.s == 3

    def edge_step():
        rows_out_copy(blocks - 1).wait()

        @pl.when(last)
        def _():
            conv_grad[:, length : length + 8, :] = jnp.zeros((seqs, 8, depth), jnp.float32)

        @pl.when(here.s > 0)
        def _():
            remote(conv_grad.at[:, 0:8], conv_grad.at[:, length : length + 8], edge_s, edge_r, (jnp.maximum(here.s - 1, 0), here.f)).start()

    def edge_wait():
        copy = remote(conv_grad.at[:, 0:8], conv_grad.at[:, length : length + 8], edge_s, edge_r, (jnp.maximum(here.s - 1, 0), here.f))

        @pl.when(here.s > 0)
        def _():
            copy.wait_send()

        @pl.when(jnp.logical_not(last))
        def _():
            copy.wait_recv()

    def gate_step(j):
        for copy in part_in(j + blocks):
            copy.wait()
        start_block(j + blocks + 1)
        slot, at = j % 2, slice(j * 256, (j + 1) * 256)
        for q in range(seqs):
            span = slice(q * length, (q + 1) * length)
            grad = sum(taps[2 - k : 3 - k, at] * conv_grad[q, k : k + length, at] for k in range(3))
            proj_back[span, at] = (grad * part[slot, 2, span, :].astype(jnp.float32)).astype(jnp.bfloat16)
            proj_back[span, 2 * depth + j * 256 : 2 * depth + (j + 1) * 256] = (grad * part[slot, 0, span, :].astype(jnp.float32)).astype(jnp.bfloat16)

    def several(*steps):
        def run():
            for step in steps:
                step()

        return run

    columns_done = width // chunk
    start_weights = lambda: weight_in(0).start()
    work = [norm_two_step]
    work += [several(*[functools.partial(conv_step, j) for j in (i, i + 1)]) for i in range(0, blocks, 2)]
    work[-1] = several(work[-1], edge_step)
    work += [several(edge_wait, *[functools.partial(gate_step, j) for j in range(blocks // 2)])]
    work += [several(*[functools.partial(gate_step, j) for j in range(blocks // 2, blocks)], start_weights)]
    work += [functools.partial(grad_in_step, j) for j in range(columns_done)]
    work += [several(lambda: block_out(columns_done - 1).wait(), functools.partial(back_step, 0))]
    work += [functools.partial(back_step, j) for j in range(1, blocks)] + [norm_step]
    work += [functools.partial(small_step, j) for j in range(4)]
    hidden_in.start()
    back_in.start()
    start_block(0)
    stages = (lambda red, t: red.stage0(t), stage1, both("2"), both("3"), both("4"), lambda red, t: red.stage5(t), lambda red, t: red.stage6(t))
    seen = [sum(p[0] == q[0] for p in plan[:i]) for i, q in enumerate(plan)]
    steps = len(plan) + len(stages) - 1
    for step in range(steps):
        for by, stage in enumerate(stages):
            if 0 <= step - by < len(plan):
                stage(reducers[plan[step - by][0]], seen[step - by])
        if step < len(work):
            work[step]()
    result_out.wait()
    for i, p in enumerate(plan):
        reducers[p[0]].to_core(seen[i]).wait_send()


def mix(grads, normed, down_in, tokens, edges, taps, gain_one, gain_two, w_in, w_out, projected, back, hidden, plan, kinds, cid):
    view = lambda g: (2, 2, 2, 2, 2, g.shape[0] // 32, g.shape[1])
    counts = [sum(p[0] == k for p in plan) for k in range(len(kinds))]
    sds = jax.ShapeDtypeStruct
    rows, depth = normed.shape
    seqs = edges.shape[0]
    outs = [sds((4,) + view(g)[5:], jnp.bfloat16) for g in [*grads, w_out, w_in]]
    outs += [sds((8, depth), jnp.float32), sds((rows, depth), jnp.float32), sds(w_out.shape, jnp.bfloat16), sds(w_in.shape, jnp.bfloat16)]
    land, scratch, sems = [], [], []
    for (height, width), count in zip(kinds, counts):
        land += landing_shapes(count, False, height, width)
        scratch += scratch_shapes(4, False, height, width)
        sems += sem_shapes(count)
    whole = pl.BlockSpec(memory_space=pltpu.VMEM)
    vmem = pltpu.VMEM
    res = pl.pallas_call(
        functools.partial(mix_kernel, plan, kinds),
        out_shape=outs + land,
        in_specs=[ANY] * len(grads) + [whole] * 7 + [ANY] * 5,
        out_specs=[ANY] * (len(grads) + 2) + [whole] + [ANY] * (3 + len(land)),
        scratch_shapes=scratch
        + sems
        + [DMA((len(kinds),)), vmem((4, 8, depth), jnp.float32), vmem((6, 8, depth), jnp.float32), DMA((6,)), DMA((6,))]
        + [vmem((depth, rows), jnp.bfloat16), vmem((depth, 768), jnp.bfloat16), vmem((2, 256, w_in.shape[1]), jnp.bfloat16)]
        + [vmem((rows, depth), jnp.float32)] * 2
        + [DMA((13,)), vmem((rows, 3 * depth), jnp.bfloat16), vmem((rows, depth), jnp.bfloat16), vmem((seqs, rows // seqs + 8, depth), jnp.float32)]
        + [vmem((2, 3, rows, 256), jnp.bfloat16), vmem((seqs, rows // seqs + 8, 256), jnp.float32), vmem((256, depth), jnp.bfloat16)]
        + [DMA, DMA],
        compiler_params=pltpu.CompilerParams(collective_id=cid, has_side_effects=True, vmem_limit_bytes=61 << 20),
        name="mix",
    )(*[g.reshape(view(g)) for g in grads], normed, down_in, tokens, edges, taps, gain_one, gain_two, w_in, w_out, projected, back, hidden)
    return res[: len(grads) + 4]


def from_behind(shard, axis, by):
    count = lax.axis_size(axis)
    pairs = [(i, i + by) for i in range(count) if 0 <= i + by < count]
    return lax.ppermute(shard, axis, pairs)


def norm_rows(token_rows, gain):
    scale = lax.rsqrt(jnp.mean(token_rows * token_rows, -1, keepdims=True) + EPS)
    unit = token_rows * scale
    return (scale, unit, (unit * gain).astype(jnp.bfloat16))


def norm_back(grad, scale, unit, gain):
    gain_grad = jnp.sum(grad * unit, 0)
    inner = grad * gain
    return (gain_grad, scale * (inner - unit * jnp.mean(inner * unit, -1, keepdims=True)))


def left_cross(left, right):
    return lax.dot_general(left, right, (((0,), (0,)), ((), ())), preferred_element_type=jnp.float32)


def against(left, weight):
    return lax.dot_general(left, weight, (((1,), (1,)), ((), ())), preferred_element_type=jnp.float32)


def product(left, right):
    return jnp.dot(left, right, preferred_element_type=jnp.float32)


def routed():
    return lax.axis_size("seq") == 4 and lax.axis_size("fsdp") == 8


def gather_all(shards, axis=0):
    return [lax.all_gather(a, "fsdp", axis=axis, tiled=True) for a in shards]


def reduce_all(grads):
    outs = []
    for g in grads:
        part = lax.psum_scatter(g.astype(jnp.bfloat16), "fsdp", scatter_dimension=0, tiled=True)
        outs.append(lax.psum(part, "seq").astype(jnp.float32))
    return outs


def plan_of(grads):
    kinds = [(48, 768), (216, 128)]
    plan = []
    for i, g in enumerate(grads):
        kind = 0 if g.shape[0] == 1536 else 1
        plan += [(kind, i, column) for column in range(0, g.shape[1], kinds[kind][1])]
    return plan, kinds


def plain(tokens, keep_mask, upstream, down_in, gain_one, conv_taps, gain_two, w_in, w_out, w_gate, w_up, w_down):
    count, block_rows, model_width = tokens.shape
    rows = count * block_rows

    def shifted(value, edge, side):
        value = value.reshape(count, block_rows, model_width)
        return jnp.concatenate([edge, value] if side < 0 else [value, edge], 1)

    def window(value, start):
        return value[:, start : start + block_rows].reshape(rows, model_width)

    token_rows = tokens.reshape(rows, model_width).astype(jnp.float32)
    scale_one, unit_one, normed_one = norm_rows(token_rows, gain_one)
    projected = product(normed_one, w_in)
    in_gate = projected[:, :model_width]
    out_gate = projected[:, model_width : 2 * model_width]
    values = projected[:, 2 * model_width :]
    mixed = in_gate * values
    edge_rows = from_behind(mixed.reshape(count, block_rows, model_width)[:, block_rows - 2 :], "seq", 1)
    extended = shifted(mixed, edge_rows, -1)
    conv_out = conv_taps[0] * window(extended, 0) + conv_taps[1] * window(extended, 1) + conv_taps[2] * window(extended, 2)
    gated = (out_gate * conv_out).astype(jnp.bfloat16)
    hidden_one = token_rows + product(gated, w_out)
    scale_two, unit_two, normed_two = norm_rows(hidden_one, gain_two)
    gate_pre = product(normed_two, w_gate)
    up_pre = product(normed_two, w_up)
    sigmoid_gate = jax.nn.sigmoid(gate_pre)
    silu_value = gate_pre * sigmoid_gate
    activated = (silu_value * up_pre).astype(jnp.bfloat16)
    hidden_two = hidden_one + product(activated, w_down)
    output = (keep_mask * hidden_two).astype(jnp.bfloat16)
    grad_down = left_cross(activated, down_in)
    grad_act = against(down_in, w_down)
    gate_back = (grad_act * up_pre * sigmoid_gate * (1.0 + gate_pre * (1.0 - sigmoid_gate))).astype(jnp.bfloat16)
    up_back = (grad_act * silu_value).astype(jnp.bfloat16)
    grad_gate = left_cross(normed_two, gate_back)
    grad_up = left_cross(normed_two, up_back)
    grad_normed_two = against(gate_back, w_gate) + against(up_back, w_up)
    grad_gain_two, through_two = norm_back(grad_normed_two, scale_two, unit_two, gain_two)
    grad_hidden = upstream + through_two
    out_back = grad_hidden.astype(jnp.bfloat16)
    grad_out = left_cross(gated, out_back)
    grad_gated = against(out_back, w_out)
    grad_out_gate = grad_gated * conv_out
    grad_conv = grad_gated * out_gate
    edge_grad = from_behind(grad_conv.reshape(count, block_rows, model_width)[:, :2], "seq", -1)
    grad_ext = shifted(grad_conv, edge_grad, 1)
    grad_mixed = conv_taps[2] * window(grad_ext, 0) + conv_taps[1] * window(grad_ext, 1) + conv_taps[0] * window(grad_ext, 2)
    grad_taps = [jnp.sum(grad_conv * window(extended, offset), 0) for offset in range(3)]
    proj_back = jnp.concatenate([grad_mixed * values, grad_out_gate, grad_mixed * in_gate], 1).astype(jnp.bfloat16)
    grad_in = left_cross(normed_one, proj_back)
    grad_normed_one = against(proj_back, w_in)
    grad_gain_one, through_one = norm_back(grad_normed_one, scale_one, unit_one, gain_one)
    tokens_grad = grad_hidden + through_one
    small_grads = jnp.stack([grad_gain_one, *grad_taps, grad_gain_two])
    return output, tokens_grad, small_grads, grad_in, grad_out, grad_gate, grad_up, grad_down


def local(tokens, lengths, norm_gain, in_weight, conv_weight, out_weight, ffn_gain, gate_weight, up_weight, down_weight, cotangent):
    count, block_rows, model_width = tokens.shape
    rows = count * block_rows
    width = norm_gain.shape[0]
    rank = lax.axis_index("fsdp")
    small = jnp.concatenate([norm_gain[None], conv_weight, ffn_gain[None]], 0).astype(jnp.float32)
    window = lambda size, start: lax.dynamic_update_slice(jnp.zeros((8, size), jnp.float32), small, (0, start))
    places = lax.axis_index("seq") * block_rows + jnp.arange(block_rows, dtype=jnp.int32)
    keep_mask = (places[None, :] < lengths[:, None]).astype(jnp.float32).reshape(rows, 1)
    upstream = cotangent.reshape(rows, model_width).astype(jnp.float32) * keep_mask
    down_in = upstream.astype(jnp.bfloat16)
    if routed():
        shards = [out_weight, in_weight, gate_weight, up_weight, down_weight]
        token_rows = tokens.reshape(rows, model_width)
        w_out, w_in, w_gate, w_up, w_down, normed_one, projected, edges, vectors, hidden_one, normed_two, mine_t, mate_t = front(shards, window(256, rank * width % 128), token_rows, 0)
        output, grad_normed_two, grad_down, ffn_sums = ffn(normed_two, mine_t, mate_t, down_in, keep_mask, w_gate, w_up, w_down, hidden_one, 1)
        grad_down, grad_out, grad_in, small_grads, tokens_grad = mix(
            [grad_down], normed_one, down_in, token_rows, edges, vectors[1:4], vectors[0:1], vectors[4:5],
            w_in, w_out, projected, grad_normed_two, hidden_one, *plan_of([grad_down, w_out, w_in]), 2,
        )[:5]
        shards = [grad_down, grad_out, grad_in, ffn_sums[0], ffn_sums[1]]
        grad_down, grad_out, grad_in, grad_gate, grad_up = [g.reshape(-1, g.shape[-1]).astype(jnp.float32) for g in shards]
    else:
        w_in, w_out, w_gate, w_up, w_down = gather_all([in_weight, out_weight, gate_weight, up_weight, down_weight])
        vectors = lax.psum(window(model_width, rank * width), "fsdp")
        output, tokens_grad, small_grads, *grads = plain(
            tokens, keep_mask, upstream, down_in, vectors[0], vectors[1:4], vectors[4], w_in, w_out, w_gate, w_up, w_down
        )
        grad_in, grad_out, grad_gate, grad_up, grad_down = reduce_all(grads)
        small_grads = lax.psum(small_grads, ("seq", "fsdp"))
    small_grads = lax.dynamic_slice_in_dim(small_grads, lax.axis_index("fsdp") * width, width, 1)
    return (
        output.reshape(tokens.shape),
        tokens_grad.reshape(tokens.shape),
        small_grads[0],
        grad_in,
        small_grads[1:4],
        grad_out,
        small_grads[4],
        grad_gate,
        grad_up,
        grad_down,
    )


def solution(mesh):
    split = P("fsdp", "seq", None)
    rows, columns, vector = P("fsdp", None), P(None, "fsdp"), P("fsdp")
    return jax.shard_map(
        local,
        mesh=mesh,
        in_specs=(split, vector, vector, rows, columns, rows, vector, rows, rows, rows, split),
        out_specs=(split, split, vector, rows, columns, rows, vector, rows, rows, rows),
        check_vma=False,
    )
```

```python
import functools

import jax
import jax.numpy as jnp
from jax import lax
from jax.experimental import pallas as pl
from jax.experimental.pallas import tpu as pltpu
from jax.sharding import PartitionSpec as P

EPS = 1e-05
MESH = pl.DeviceIdType.MESH

DMA = pltpu.SemaphoreType.DMA
ANY = pl.BlockSpec(memory_space=pl.ANY)


def rem(t, n):
    return t % n if isinstance(t, int) else lax.rem(t, n)


def remote(src, dst, send, recv, to):
    return pltpu.make_async_remote_copy(src_ref=src, dst_ref=dst, send_sem=send, recv_sem=recv, device_id=to, device_id_type=MESH)


class Here:
    def __init__(self):
        s, f = lax.axis_index("seq"), lax.axis_index("fsdp")
        self.s, self.f = s, f
        self.z, self.c = f // 2, lax.rem(f, 2)
        self.s0, self.s1 = lax.rem(s, 2), s // 2
        self.mate = (s, f + 1 - 2 * self.c)
        self.beside = (s + 1 - 2 * self.s0, s + 2 - 4 * self.s1)

    def greet(self, along=False):
        barrier = pltpu.get_barrier_semaphore()
        peers = [self.mate] + [(b, self.f) for b in self.beside] + [(self.s, lax.rem(self.f + 2 * j, 8)) for j in (1, 2, 3)]
        for peer in peers:
            pl.semaphore_signal(barrier, inc=1, device_id=peer, device_id_type=MESH)
        count = len(peers)
        if along:
            before, after = self.s > 0, self.s < 3
            for there, step in ((before, -1), (after, 1)):

                @pl.when(there)
                def _(step=step):
                    pl.semaphore_signal(barrier, inc=1, device_id=(jnp.clip(self.s + step, 0, 3), self.f), device_id_type=MESH)

            count = count + jnp.where(before, 1, 0) + jnp.where(after, 1, 0)
        pl.semaphore_wait(barrier, count)


class Reducer:
    def __init__(self, here, paired, held, total, fresh, landing, sems, core_source, goal):
        self.here, self.paired = here, paired
        self.held, self.fresh, self.total, self.landing = held, fresh, total, landing
        (self.local, self.core_s, self.core_r, self.one_s, self.one_r, self.two_s, self.two_r) = sems[:7]
        (self.z_s, self.z_r, self.near_s, self.near_r, self.far_s, self.far_r) = sems[7:]
        self.core_source, self.goal = core_source, goal
        self.slots, self.chips = held.shape[0], held.shape[2]

    def mine(self, t):
        return self.held.at[rem(t, self.slots)]

    def to_core(self, t):
        return remote(self.core_source(t), self.landing[0].at[t], self.core_s.at[t], self.core_r.at[t], self.here.mate)

    def one(self, t, d):
        h = self.here
        src = self.mine(t).at[0, :, :, 1 - h.s0] if d == 0 else self.mine(t).at[1, :, 1 - h.s1]
        return remote(src, self.landing[1 + d].at[t], self.one_s.at[t, d], self.one_r.at[t, d], (h.beside[d], h.f))

    def two(self, t, d):
        h = self.here
        src = self.mine(t).at[1, :, h.s1, 1 - h.s0] if d == 0 else self.mine(t).at[0, :, 1 - h.s1, h.s0]
        return remote(src, self.landing[4 - d].at[t], self.two_s.at[t, d], self.two_r.at[t, d], (h.beside[d], h.f))

    def part(self, t, a):
        h = self.here
        if self.paired:
            return self.mine(t).at[:, a, h.s1, h.s0]
        return self.mine(t).at[a // 2, lax.rem(a, 2), h.s1, h.s0]

    def to_chip(self, t, j):
        h = self.here
        a = lax.rem(h.z + j, 4)
        slot = jnp.where(h.z < a, h.z, h.z - 1)
        return remote(self.part(t, a), self.landing[5].at[t, slot], self.z_s.at[t, j - 1], self.z_r.at[t, slot], (h.s, 2 * a + h.c))

    def from_chip(self, t, slot):
        h = self.here
        return remote(self.part(t, 0), self.landing[5].at[t, slot], self.z_s.at[t, 0], self.z_r.at[t, slot], h.mate)

    def keep(self, t):
        return pltpu.make_async_copy(self.total.at[rem(t, 2)], self.goal(t, self.here.s, None), self.local.at[8 + rem(t, 2)])

    def near(self, t, d):
        h = self.here
        return remote(self.total.at[rem(t, 2)], self.goal(t, h.s, None), self.near_s.at[t, d], self.near_r.at[t, d], (h.beside[d], h.f))

    def far(self, t, d):
        h = self.here
        ref = self.goal(t, h.beside[1 - d], d)
        return remote(ref, ref, self.far_s.at[t, d], self.far_r.at[t, d], (h.beside[d], h.f))

    def pending(self, src, dst, which):
        return pltpu.make_async_copy(src, dst, self.local.at[which])

    def bring(self, src, dst, which):
        self.pending(src, dst, which).start()

    def stage0(self, t):
        self.to_core(t).start()

    def fetch1(self, t):
        self.to_core(t).wait_recv()
        self.bring(self.landing[0].at[t], self.fresh[0], 0)

    def stage1(self, t):
        fresh, me = self.fresh[0], self.mine(t)
        self.pending(self.landing[0].at[t], fresh, 0).wait()

        @pl.loop(0, 2 * self.chips)
        def _(i):
            at = (i // self.chips, lax.rem(i, self.chips))
            me[at] = me[at] + fresh[at]

        self.one(t, 0).start()
        self.one(t, 1).start()

    def fetch2(self, t):
        for d in (0, 1):
            self.one(t, d).wait_recv()
            self.bring(self.landing[1 + d].at[t], self.fresh[1].at[d], 1 + d)

    def stage2(self, t):
        h, fresh, me = self.here, self.fresh[1], self.mine(t)
        for d in (0, 1):
            self.pending(self.landing[1 + d].at[t], fresh.at[d], 1 + d).wait()

        @pl.loop(0, self.chips)
        def _(a):
            for b in (0, 1):
                me[0, a, b, h.s0] = me[0, a, b, h.s0] + fresh[0, a, b]
                me[1, a, h.s1, b] = me[1, a, h.s1, b] + fresh[1, a, b]

        self.two(t, 1).start()
        self.two(t, 0).start()

    def fetch3(self, t):
        for d in (1, 0):
            self.two(t, d).wait_recv()
            self.bring(self.landing[4 - d].at[t], self.fresh[2].at[1 - d], 4 - d)

    def stage3(self, t):
        h, fresh, me = self.here, self.fresh[2], self.mine(t)
        for d in (1, 0):
            self.pending(self.landing[4 - d].at[t], fresh.at[1 - d], 4 - d).wait()

        @pl.loop(0, self.chips)
        def _(a):
            me[0, a, h.s1, h.s0] = me[0, a, h.s1, h.s0] + fresh[0, a]
            me[1, a, h.s1, h.s0] = me[1, a, h.s1, h.s0] + fresh[1, a]

        for j in (1, 2, 3):
            self.to_chip(t, j).start()

    def fetch4(self, t):
        for slot in range(3):
            self.from_chip(t, slot).wait_recv()
            self.bring(self.landing[5].at[t, slot], self.fresh[3].at[slot], 5 + slot)

    def stage4(self, t):
        h, fresh = self.here, self.fresh[3]
        for slot in range(3):
            self.pending(self.landing[5].at[t, slot], fresh.at[slot], 5 + slot).wait()
        acc = self.part(t, h.z)[...].astype(jnp.float32)
        for slot in range(3):
            acc += fresh[slot].astype(jnp.float32)
        self.total[rem(t, 2)] = acc.astype(jnp.bfloat16)
        self.near(t, 0).start()
        self.near(t, 1).start()
        self.keep(t).start()
        for d in (0, 1):
            self.one(t, d).wait_send()
            self.two(t, d).wait_send()
        for j in (1, 2, 3):
            self.to_chip(t, j).wait_send()

    def near_in(self, t, d):
        h = self.here
        ref = self.goal(t, h.beside[d], None)
        return remote(ref, ref, self.near_s.at[t, d], self.near_r.at[t, d], (h.beside[d], h.f))

    def far_in(self, t, d):
        h = self.here
        ref = self.goal(t, 3 - h.s, d)
        return remote(ref, ref, self.far_s.at[t, d], self.far_r.at[t, d], (h.beside[d], h.f))

    def stage5(self, t):
        self.near_in(t, 1).wait_recv()
        self.far(t, 0).start()
        self.near_in(t, 0).wait_recv()
        self.far(t, 1).start()
        self.near(t, 0).wait_send()
        self.near(t, 1).wait_send()
        self.keep(t).wait()

    def stage6(self, t):
        for d in (0, 1):
            self.far_in(t, d).wait_recv()
            self.far(t, d).wait_send()


def landing_shapes(n, paired, rows, width):
    chips = 4 if paired else 2
    lead = (2,) if paired else ()
    shapes = [(n, 2, chips, 2, 2, rows, width)] + [(n, chips, 2, rows, width)] * 2 + [(n, chips, rows, width)] * 2 + [(n, 3) + lead + (rows, width)]
    return [jax.ShapeDtypeStruct(shape, jnp.bfloat16) for shape in shapes]


def scratch_shapes(slots, paired, rows, width):
    chips = 4 if paired else 2
    lead = (2,) if paired else ()
    shapes = [(slots, 2, chips, 2, 2, rows, width), (2,) + lead + (rows, width)]
    shapes += [(2, chips, 2, 2, rows, width), (2, chips, 2, rows, width), (2, chips, rows, width), (3,) + lead + (rows, width)]
    return [pltpu.VMEM(shape, jnp.bfloat16) for shape in shapes]


def sem_shapes(n):
    return [DMA((10,)), DMA((n,)), DMA((n,))] + [DMA((n, 2))] * 4 + [DMA((n, 3))] * 2 + [DMA((n, 2))] * 4


def halves(rows):
    half = (rows // 2 + 7) // 8 * 8
    return {None: pl.ds(0, rows), 0: pl.ds(0, half), 1: pl.ds(half, rows - half)}


TILE = 256
SUBS = 3
SLOTS = 5


def dot_nn(a, b):
    return lax.dot_general(a, b, (((1,), (0,)), ((), ())), preferred_element_type=jnp.float32)


def dot_nt(a, b):
    return lax.dot_general(a, b, (((1,), (1,)), ((), ())), preferred_element_type=jnp.float32)


def dot_tn(a, b):
    return lax.dot_general(a, b, (((0,), (0,)), ((), ())), preferred_element_type=jnp.float32)


def ffn_kernel(tiles, n2, mine_t, mate_t, down_in, keep, w_gate, w_up, w_down, hidden, *refs):
    output, back, grad_down, shards = refs[:4]
    landing = refs[4:10]
    act, gate_back, up_back, outgoing, held, total = refs[10:16]
    fresh, sems = refs[16:20], refs[20:33]
    y, start_sem = refs[33:]
    hidden_in = pltpu.make_async_copy(hidden, y, start_sem)
    i = pl.program_id(0)
    chunks = tiles // SUBS
    here = Here()
    width = TILE * SUBS
    rows = shards.shape[2]
    spans = halves(rows)

    def goal(t, quarter, part):
        return shards.at[:, quarter, spans[part], pl.ds(pl.multiple_of(t * width, width), width)]

    red = Reducer(here, True, held, total, fresh, landing, sems, lambda t: outgoing.at[lax.rem(t, 2)], goal)

    def hook(offset, *stages):
        past = i - offset
        t = past // SUBS

        @pl.when((past >= 0) & (lax.rem(past, SUBS) == 0) & (t < chunks))
        def _():
            for stage in stages:
                stage(t)

    @pl.when(i == 0)
    def _():
        here.greet()
        hidden_in.start()
        back[...] = jnp.zeros_like(back)

    @pl.when(i < tiles)
    def _():
        g = dot_nn(n2[...], w_gate[...])
        u = dot_nn(n2[...], w_up[...])
        a = dot_nt(down_in[...], w_down[...])
        sig = jax.nn.sigmoid(g)
        silu = g * sig
        act[...] = (silu * u).astype(jnp.bfloat16)
        gate_back[...] = (a * u * (sig * (1.0 + g * (1.0 - sig)))).astype(jnp.bfloat16)
        up_back[...] = (a * silu).astype(jnp.bfloat16)

    hook(7, red.stage2)
    hook(13, red.fetch4)

    @pl.when(i == 0)
    def _():
        hidden_in.wait()

    @pl.when(i == tiles)
    def _():
        output[...] = (y[...] * keep[...]).astype(jnp.bfloat16)

    @pl.when(i < tiles)
    def _():
        @pl.loop(0, 3)
        def _(j):
            at = pl.ds(pl.multiple_of(j * 512, 512), 512)
            y[:, at] += dot_nn(act[...], w_down[:, at])
            back[:, at] += dot_nt(gate_back[...], w_gate[at, :]) + dot_nt(up_back[...], w_up[at, :])
            grad_down[:, at] = dot_tn(act[...], down_in[:, at]).astype(jnp.bfloat16)

    hook(3, red.fetch1)
    hook(10, red.fetch3)
    chunk, sub = i // SUBS, lax.rem(i, SUBS)

    @pl.when((sub == 0) & (chunk >= 2) & (chunk < chunks + 2))
    def _():
        red.to_core(chunk - 2).wait_send()

    @pl.when(i < tiles)
    def _():
        at = pl.ds(pl.multiple_of(sub * TILE, TILE), TILE)
        out, me = outgoing.at[lax.rem(chunk, 2)], red.mine(chunk)
        shape = (4, 2, 2, rows, TILE)
        for m, grad in ((0, gate_back), (1, up_back)):
            out[m, :, :, :, :, at] = dot_nn(mate_t[...], grad[...]).astype(jnp.bfloat16).reshape(shape)
            me[m, :, :, :, :, at] = dot_nn(mine_t[...], grad[...]).astype(jnp.bfloat16).reshape(shape)

    hook(3, red.stage1)
    hook(6, red.fetch2)
    hook(10, red.stage3)
    hook(13, red.stage4)
    hook(16, red.stage5)
    hook(19, red.stage6)

    @pl.when((sub == SUBS - 1) & (chunk < chunks))
    def _():
        red.stage0(chunk)


def ffn(n2, mine_t, mate_t, down_in, keep, w_gate, w_up, w_down, hidden_one, cid):
    m, d = n2.shape
    hidden = w_gate.shape[1]
    tiles = hidden // TILE
    chunks, width = tiles // SUBS, TILE * SUBS
    rows = d // 32
    one = lambda *shape: pl.BlockSpec(shape, lambda i: (0, 0), pipeline_mode=pl.Buffered(1))
    across = pl.BlockSpec((d, TILE), lambda i: (0, jnp.minimum(i, tiles - 1)))
    down = pl.BlockSpec((TILE, d), lambda i: (jnp.minimum(i, tiles - 1), 0))
    out_shape = [jax.ShapeDtypeStruct((m, d), jnp.bfloat16), jax.ShapeDtypeStruct((m, d), jnp.float32)] + [jax.ShapeDtypeStruct((hidden, d), jnp.bfloat16), jax.ShapeDtypeStruct((2, 4, rows, hidden), jnp.bfloat16)]
    out_shape += landing_shapes(chunks, True, rows, width)
    res = pl.pallas_call(
        functools.partial(ffn_kernel, tiles),
        grid=(tiles + 17,),
        out_shape=out_shape,
        in_specs=[one(m, d), one(d // 2, m), one(d // 2, m), one(m, d), one(m, 1), across, across, down, ANY],
        out_specs=[one(m, d), one(m, d), down, ANY] + [ANY] * 6,
        scratch_shapes=[pltpu.VMEM((m, TILE), jnp.bfloat16)] * 3
        + [pltpu.VMEM((2, 2, 4, 2, 2, rows, width), jnp.bfloat16)]
        + scratch_shapes(SLOTS, True, rows, width)
        + sem_shapes(chunks)
        + [pltpu.VMEM((m, d), jnp.float32), DMA],
        compiler_params=pltpu.CompilerParams(collective_id=cid, has_side_effects=True, vmem_limit_bytes=61 << 20),
        name="ffn",
    )(n2, mine_t, mate_t, down_in, keep, w_gate, w_up, w_down, hidden_one)
    return res[:4]


def front_kernel(count, *refs):
    shards, small, tokens = refs[:count], refs[count], refs[count + 1]
    at = count + 2
    fulls = refs[at : at + count]
    normed_one, projected, edges, vectors, hidden_out, normed_two, mine_t, mate_t = refs[at + count : at + count + 8]
    at += count + 8
    (local_sem, core_send, core_recv, z_send, z_recv, near_send, near_recv, far_send, far_recv, small_send, small_recv) = refs[at : at + 11]
    at += 11
    staged = refs[at : at + count]
    smalls, weights, part, mixed, gated, hidden, turned, work_sem, edge_s, edge_r = refs[at + count :]
    s, f = lax.axis_index("seq"), lax.axis_index("fsdp")
    z, c = f // 2, lax.rem(f, 2)
    mate = f + 1 - 2 * c
    beside = (s + 1 - 2 * lax.rem(s, 2), s + 2 - 4 * (s // 2))
    last = 3
    flip = z >= 2
    zf = jnp.where(flip, last - z, z)

    def source(j):
        a = jnp.where(j < zf, j, j + 1)
        return jnp.where(flip, last - a, a)

    def slot(at, a):
        turned = at >= 2
        at = jnp.where(turned, last - at, at)
        a = jnp.where(turned, last - a, a)
        return jnp.where(a < at, a, a - 1)

    barrier = pltpu.get_barrier_semaphore()
    for k in range(1, 8):
        pl.semaphore_signal(barrier, inc=1, device_id=(s, lax.rem(f + k, 8)), device_id_type=MESH)
    for b in beside:
        pl.semaphore_signal(barrier, inc=1, device_id=(b, f), device_id_type=MESH)
    before, after = s > 0, s < 3
    for there, step in ((before, -1), (after, 1)):

        @pl.when(there)
        def _(step=step):
            pl.semaphore_signal(barrier, inc=1, device_id=(jnp.clip(s + step, 0, 3), f), device_id_type=MESH)

    pl.semaphore_wait(barrier, 9 + jnp.where(before, 1, 0) + jnp.where(after, 1, 0))

    def remote(src, dst, send, recv, to):
        return pltpu.make_async_remote_copy(src_ref=src, dst_ref=dst, send_sem=send, recv_sem=recv, device_id=to, device_id_type=MESH)

    def rows(m, shard_index, quarter=None, part=None):
        r = shards[m].shape[0]
        start, size = shard_index * r, r
        if quarter is not None:
            size = r // 4
            start = start + quarter * size
            half = (size // 2 + 7) // 8 * 8
            if part == 0:
                size = half
            elif part == 1:
                start, size = start + half, size - half
        return pl.ds(pl.multiple_of(start, 8), size)

    def place(m, *where):
        return fulls[m].at[rows(m, *where)]

    def load(m):
        return pltpu.make_async_copy(shards[m], staged[m], local_sem.at[m])

    def keep(m):
        return pltpu.make_async_copy(staged[m], place(m, f), local_sem.at[m])

    def own_core(m):
        return remote(shards[m], place(m, f), core_send.at[m, 3], core_recv.at[m, 3], (s, mate))

    def z_own(m, up):
        to = z + 1 if up else z - 1
        return remote(shards[m].at[rows(m, 0, s)], place(m, f, s), z_send.at[m, 3 + up], z_recv.at[m, slot(to, z)], (s, 2 * to + c))

    def z_on(m, j):
        a = source(j)
        to = jnp.where(a < z, z + 1, z - 1)
        at = place(m, 2 * a + c, s)
        to_safe = jnp.clip(to, 0, last)
        return remote(at, at, z_send.at[m, j], z_recv.at[m, jnp.clip(slot(to_safe, a), 0, 2)], (s, 2 * to_safe + c))

    def z_in(m, j):
        at = place(m, 2 * source(j) + c, s)
        return remote(at, at, z_send.at[m, j], z_recv.at[m, j], (s, f))

    def goes_on(j):
        a = source(j)
        return jnp.where(a < z, z < last, z > 0)

    def near(m, j, d):
        at = place(m, 2 * source(j) + c, s)
        return remote(at, at, near_send.at[m, j, d], near_recv.at[m, j, d], (beside[d], f))

    def far(m, j, d):
        at = place(m, 2 * source(j) + c, beside[1 - d], d)
        return remote(at, at, far_send.at[m, j, d], far_recv.at[m, j, d], (beside[d], f))

    def core(m, j):
        at = place(m, 2 * source(j) + c)
        return remote(at, at, core_send.at[m, j], core_recv.at[m, j], (s, mate))

    def begin(m):
        @pl.when(z < last)
        def _():
            z_own(m, 1).start()
        @pl.when(z > 0)
        def _():
            z_own(m, 0).start()
        load(m).start()
        own_core(m).start()

    def spread(m, j):
        z_in(m, j).wait_recv()
        @pl.when(goes_on(j))
        def _():
            z_on(m, j).start()
        near(m, j, 0).start()
        near(m, j, 1).start()
        if j == 0:
            load(m).wait()
            keep(m).start()

    def diagonal(m, j):
        near(m, j, 1).wait_recv()
        far(m, j, 0).start()
        near(m, j, 0).wait_recv()
        far(m, j, 1).start()

    def share(m, j):
        far(m, j, 0).wait_recv()
        far(m, j, 1).wait_recv()
        core(m, j).start()

    def finish(m, j):
        if j == 0:
            keep(m).wait()
            own_core(m).wait()
            @pl.when(z < last)
            def _():
                z_own(m, 1).wait_send()
            @pl.when(z > 0)
            def _():
                z_own(m, 0).wait_send()
        @pl.when(goes_on(j))
        def _():
            z_on(m, j).wait_send()
        for d in (0, 1):
            near(m, j, d).wait_send()
            far(m, j, d).wait_send()
        core(m, j).wait()

    def small_copy(k):
        return remote(small, smalls.at[f], small_send.at[k - 1], small_recv.at[k - 1], (s, lax.rem(f + k, 8)))

    depth = tokens.shape[1]
    blocks = depth // 256
    seqs, length = mixed.shape[0], mixed.shape[1] - 8
    gain_one, taps, gain_two = 0, 1, 4

    def small_step():
        vectors[...] = jnp.zeros(vectors.shape, jnp.float32)
        for k in range(8):
            if k:
                small_copy(k).wait()
            start = lax.rem(f + 8 - k, 8) * (depth // 8) // 128 * 128
            at = pl.ds(pl.multiple_of(start, 128), small.shape[1])
            vectors[:, at] = vectors[:, at] + (smalls[k - 1] if k else small[...])

    def norm_one_step():
        @pl.loop(0, tokens.shape[0] // 64)
        def _(r):
            at = pl.ds(pl.multiple_of(r * 64, 64), 64)
            token_rows = tokens[at, :].astype(jnp.float32)
            scale = lax.rsqrt(jnp.mean(token_rows * token_rows, -1, keepdims=True) + EPS)
            normed_one[at, :] = (token_rows * scale * vectors[gain_one : gain_one + 1, :]).astype(jnp.bfloat16)

    def weight_in(j):
        slot = j % 2
        return [
            pltpu.make_async_copy(fulls[1].at[:, pl.ds(g * depth + j * 256, 256)], weights.at[slot, g], work_sem.at[3 * slot + g])
            for g in range(3)
        ]

    def part_out(j):
        slot = j % 2
        return [
            pltpu.make_async_copy(part.at[slot, g], projected.at[:, pl.ds(g * depth + j * 256, 256)], work_sem.at[6 + 3 * slot + g])
            for g in range(3)
        ]

    def start_all(copies):
        for copy in copies:
            copy.start()

    def wait_all(copies):
        for copy in copies:
            copy.wait()

    def project_step(j):
        slot, at = j % 2, slice(j * 256, (j + 1) * 256)
        if j == 0:
            start_all(weight_in(0))
        wait_all(weight_in(j))
        if j + 1 < blocks:
            start_all(weight_in(j + 1))
        if j >= 2:
            wait_all(part_out(j - 2))
        for g in range(3):
            part[slot, g] = dot_nn(normed_one[...], weights[slot, g]).astype(jnp.bfloat16)
        start_all(part_out(j))
        gated[:, at] = part[slot, 1]
        for q in range(seqs):
            span = slice(q * length, (q + 1) * length)
            mixed[q, 8:, at] = part[slot, 0, span, :].astype(jnp.float32) * part[slot, 2, span, :].astype(jnp.float32)

    def edge_copy():
        return remote(mixed.at[:, length : length + 8], mixed.at[:, 0:8], edge_s, edge_r, (jnp.minimum(s + 1, 3), f))

    def edge_start():
        wait_all(part_out(blocks - 2))
        wait_all(part_out(blocks - 1))

        @pl.when(jnp.logical_not(before))
        def _():
            mixed[:, 0:8, :] = jnp.zeros((seqs, 8, depth), jnp.float32)

        @pl.when(after)
        def _():
            edge_copy().start()

        start_all([out_in(0)])

    def edge_wait():
        @pl.when(after)
        def _():
            edge_copy().wait_send()

        @pl.when(before)
        def _():
            edge_copy().wait_recv()

        edges[...] = mixed[:, 0:8, :]

    def conv_step(j):
        at = slice(j * 256, (j + 1) * 256)
        for q in range(seqs):
            span = slice(q * length, (q + 1) * length)
            conv = sum(vectors[taps + k : taps + k + 1, at] * mixed[q, 6 + k : 6 + k + length, at] for k in range(3))
            gated[span, at] = (gated[span, at].astype(jnp.float32) * conv).astype(jnp.bfloat16)

    def out_in(j):
        return pltpu.make_async_copy(fulls[0].at[:, pl.ds(j * 256, 256)], weights.at[j % 2, 0], work_sem.at[3 * (j % 2)])

    def out_step(j):
        at = slice(j * 256, (j + 1) * 256)
        out_in(j).wait()
        if j + 1 < blocks:
            out_in(j + 1).start()
        hidden[:, at] = tokens[:, at].astype(jnp.float32) + dot_nn(gated[...], weights[j % 2, 0])

    hidden_copy = pltpu.make_async_copy(hidden, hidden_out, work_sem.at[12])

    def norm_two_step():
        hidden_copy.start()

        @pl.loop(0, tokens.shape[0] // 64)
        def _(r):
            at = pl.ds(pl.multiple_of(r * 64, 64), 64)
            rows_two = hidden[at, :]
            scale = lax.rsqrt(jnp.mean(rows_two * rows_two, -1, keepdims=True) + EPS)
            normed_two[at, :] = (rows_two * scale * vectors[gain_two : gain_two + 1, :]).astype(jnp.bfloat16)

    shard = depth // 8

    def turned_out():
        copies = []
        for chip in range(4):
            for goal, core_of, sem in ((mine_t, c, 0), (mate_t, 1 - c, 4)):
                start = pl.multiple_of((2 * chip + core_of) * shard, 16)
                copies.append(pltpu.make_async_copy(turned.at[pl.ds(start, shard)], goal.at[pl.ds(chip * shard, shard)], work_sem.at[sem + chip]))
        return copies

    def turn_step():
        @pl.loop(0, blocks)
        def _(r):
            at = pl.ds(pl.multiple_of(r * 256, 256), 256)
            turned[at, :] = normed_two[:, at].T

        start_all(turned_out())

    def each(step, *js):
        return [functools.partial(step, j) for j in js]

    work = {3: [small_step], 5: [norm_one_step]}
    first = 3 * 2 + 5
    work[first] = each(project_step, 0, 1)
    work[first + 1] = each(project_step, 2, 3)
    work[first + 2] = each(project_step, 4, 5) + [edge_start]
    work[first + 3] = [edge_wait] + each(conv_step, *range(blocks))
    work[first + 4] = each(out_step, *range(blocks))
    work[first + 5] = [norm_two_step, turn_step]

    def small_copy(k):
        return remote(small, smalls.at[k - 1], small_send.at[k - 1], small_recv.at[k - 1], (s, lax.rem(f + k, 8)))

    begin(0)
    for k in range(1, 8):
        small_copy(k).start()
    stages = (spread, diagonal, share, finish)
    lag = (0, 1, 3, 5)
    for step in range(3 * count + lag[-1]):
        for stage, by in zip(stages, lag):
            if 0 <= step - by < 3 * count:
                m, j = divmod(step - by, 3)
                stage(m, j)
                if stage is spread and j == 1 and m + 1 < count:
                    begin(m + 1)
        for piece in work.get(step, []):
            piece()
    hidden_copy.wait()
    wait_all(turned_out())


def front(shards, small, tokens, cid):
    count = len(shards)
    anyspec = pl.BlockSpec(memory_space=pl.ANY)
    whole = pl.BlockSpec(memory_space=pltpu.VMEM)
    vmem = pltpu.VMEM
    dma = pltpu.SemaphoreType.DMA
    sds = jax.ShapeDtypeStruct
    rows, depth = tokens.shape
    half, full = jnp.bfloat16, jnp.float32
    outs = [sds((8 * a.shape[0], a.shape[1]), a.dtype) for a in shards]
    outs += [sds((rows, depth), half), sds((rows, 3 * depth), half), sds((2, 8, depth), full), sds((8, depth), full), sds((rows, depth), full)]
    outs += [sds((rows, depth), half), sds((depth // 2, rows), half), sds((depth // 2, rows), half)]
    return pl.pallas_call(
        functools.partial(front_kernel, count),
        out_shape=outs,
        in_specs=[anyspec] * count + [whole] * 2,
        out_specs=[anyspec] * count + [whole, anyspec, whole, whole, anyspec, whole, anyspec, anyspec],
        scratch_shapes=[dma((count,)), dma((count, 4)), dma((count, 4)), dma((count, 5)), dma((count, 3))]
        + [dma((count, 3, 2))] * 4
        + [dma((7,)), dma((7,))]
        + [vmem(a.shape, a.dtype) for a in shards]
        + [vmem((7,) + small.shape, full), vmem((2, 3, depth, 256), half), vmem((2, 3, rows, 256), half), vmem((2, rows // 2 + 8, depth), full)]
        + [vmem((rows, depth), half), vmem((rows, depth), full), vmem((depth, rows), half), dma((13,)), dma, dma],
        compiler_params=pltpu.CompilerParams(collective_id=cid, has_side_effects=True, vmem_limit_bytes=58 << 20),
        name="front",
    )(*shards, small, tokens)


def mix_kernel(plan, kinds, *refs):
    arrays, n = max(p[1] for p in plan) + 1, len(kinds)
    grads = list(refs[: arrays - 2])
    normed, down_in, tokens, edges, taps, gain_one, gain_two, w_in, w_out, projected, back, hidden = refs[arrays - 2 : arrays + 10]
    at = arrays + 10
    outs, small_out, tokens_grad, grad_out, grad_in = refs[at : at + arrays], *refs[at + arrays : at + arrays + 4]
    at += arrays + 4
    grads += [grad_out, grad_in]
    landing = [refs[at + 6 * k : at + 6 * k + 6] for k in range(n)]
    at += 6 * n
    scratch = [refs[at + 6 * k : at + 6 * k + 6] for k in range(n)]
    at += 6 * n
    sems = [refs[at + 13 * k : at + 13 * k + 13] for k in range(n)]
    at += 13 * n
    own_sem, small_own, small_land, small_s, small_r, normed_t, block, weights, normed_grad, residual, work_sem = refs[at : at + 11]
    proj_back, out_back, conv_grad, part, mixed, edge_s, edge_r = refs[at + 11 :]
    here = Here()
    here.greet(True)

    def columns(k, t):
        return [p for p in plan if p[0] == k][t]

    reducers = []
    for k, (rows, width) in enumerate(kinds):
        spans = halves(rows)

        def source(t, core, k=k, width=width):
            _, array, column = columns(k, t)
            if array >= arrays - 2:
                whole = grads[array].shape
                return grads[array].reshape(2, 2, 2, 2, 2, whole[0] // 32, whole[1]).at[:, :, core, :, :, :, pl.ds(column, width)]
            return grads[array].at[:, :, core, :, :, :, pl.ds(column, width)]

        def goal(t, quarter, part, k=k, width=width, spans=spans):
            _, array, column = columns(k, t)
            return outs[array].at[quarter, spans[part], pl.ds(column, width)]

        held, total, *fresh = scratch[k]
        red = Reducer(here, False, held, total, fresh, landing[k], sems[k], lambda t, source=source: source(t, 1 - here.c), goal)
        red.own = lambda t, k=k, source=source, red=red: pltpu.make_async_copy(source(t, here.c), red.mine(t), own_sem.at[k])
        reducers.append(red)

    def ahead(red, t):
        red.own(t).start()
        red.fetch1(t)

    def stage1(red, t):
        red.own(t).wait()
        red.stage1(t)

    hops = [here.mate, (here.beside[0], here.f), (here.beside[1], here.f)]

    def small_hop(j):
        return remote(small_own.at[j], small_land.at[j], small_s.at[j], small_r.at[j], hops[j])

    def small_chip(j):
        a = lax.rem(here.z + j, 4)
        return remote(small_own.at[3], small_land.at[2 + j], small_s.at[2 + j], small_r.at[2 + j], (here.s, 2 * a + here.c))

    def small_step(j):
        if j < 3:
            small_hop(j).wait()
            small_own[j + 1] = small_own[j] + small_land[j]
            if j < 2:
                small_hop(j + 1).start()
            else:
                for i in (1, 2, 3):
                    small_chip(i).start()
        else:
            for i in (1, 2, 3):
                small_chip(i).wait()
            small_out[...] = small_own[3] + small_land[3] + small_land[4] + small_land[5]

    width, depth = proj_back.shape[1], normed.shape[1]
    chunk = block.shape[1]

    def block_out(j):
        return pltpu.make_async_copy(block, grad_in.at[:, pl.ds(j * chunk, chunk)], work_sem.at[0])

    def turn():
        @pl.loop(0, depth // 256)
        def _(r):
            at = pl.ds(pl.multiple_of(r * 256, 256), 256)
            normed_t[at, :] = normed[:, at].T

    def grad_in_step(j):
        if j == 0:
            turn()
        else:
            block_out(j - 1).wait()

        @pl.loop(0, depth // 256)
        def _(r):
            at = pl.ds(pl.multiple_of(r * 256, 256), 256)
            block[at, :] = dot_nn(normed_t[at, :], proj_back[:, j * chunk : (j + 1) * chunk]).astype(jnp.bfloat16)

        block_out(j).start()

    blocks = depth // 256

    def weight_in(j):
        return pltpu.make_async_copy(w_in.at[pl.ds(j * 256, 256)], weights.at[j % 2], work_sem.at[1 + j % 2])

    hidden_in = pltpu.make_async_copy(hidden, residual, work_sem.at[3])
    back_in = pltpu.make_async_copy(back, normed_grad, work_sem.at[4])
    result_out = pltpu.make_async_copy(normed_grad, tokens_grad, work_sem.at[3])

    def back_step(j):
        weight_in(j).wait()
        if j + 1 < blocks:
            weight_in(j + 1).start()
        normed_grad[:, j * 256 : (j + 1) * 256] = dot_nt(proj_back[...], weights[j % 2])

    def norm_step():
        @pl.loop(0, normed.shape[0] // 64)
        def _(r):
            at = pl.ds(pl.multiple_of(r * 64, 64), 64)
            token_rows = tokens[at, :].astype(jnp.float32)
            scale = lax.rsqrt(jnp.mean(token_rows * token_rows, -1, keepdims=True) + EPS)
            unit = token_rows * scale
            grad = normed_grad[at, :]
            small_own[0, 0:1, :] += jnp.sum(grad * unit, 0, keepdims=True)
            inner = grad * gain_one[...]
            normed_grad[at, :] = residual[at, :] + scale * (inner - unit * jnp.mean(inner * unit, -1, keepdims=True))

        result_out.start()
        small_hop(0).start()

    def norm_two_step():
        hidden_in.wait()
        back_in.wait()
        small_own[0] = jnp.zeros(small_own.shape[1:], jnp.float32)

        @pl.loop(0, normed.shape[0] // 64)
        def _(r):
            at = pl.ds(pl.multiple_of(r * 64, 64), 64)
            rows_two = residual[at, :]
            scale = lax.rsqrt(jnp.mean(rows_two * rows_two, -1, keepdims=True) + EPS)
            unit = rows_two * scale
            grad = normed_grad[at, :]
            small_own[0, 4:5, :] += jnp.sum(grad * unit, 0, keepdims=True)
            inner = grad * gain_two[...]
            total = down_in[at, :].astype(jnp.float32) + scale * (inner - unit * jnp.mean(inner * unit, -1, keepdims=True))
            residual[at, :] = total
            out_back[at, :] = total.astype(jnp.bfloat16)

    seqs, length = mixed.shape[0], mixed.shape[1] - 8

    def part_in(j):
        slot = j % 2
        return [
            pltpu.make_async_copy(projected.at[:, pl.ds(g * depth + (j % blocks) * 256, 256)], part.at[slot, g], work_sem.at[5 + 3 * slot + g])
            for g in range(3)
        ]

    def out_weight_in(j):
        return pltpu.make_async_copy(w_out.at[pl.ds(j * 256, 256)], weights.at[j % 2, :, 0:depth], work_sem.at[11 + j % 2])

    def rows_out(j):
        return [
            pltpu.make_async_copy(block.at[pl.ds(h * 256, 256)], grad_out.at[pl.ds(j * 256, 256), pl.ds(h * chunk, chunk)], work_sem.at[13 * h])
            for h in (0, 1)
        ]

    def start_block(j):
        if j < 2 * blocks:
            for copy in part_in(j):
                copy.start()
        if j < blocks:
            out_weight_in(j).start()

    def conv_step(j):
        for copy in part_in(j):
            copy.wait()
        out_weight_in(j).wait()
        start_block(j + 1)
        slot, at = j % 2, slice(j * 256, (j + 1) * 256)
        gated_grad = dot_nt(out_back[...], weights[slot, :, 0:depth])
        if j:
            for copy in rows_out(j - 1):
                copy.wait()
        for q in range(seqs):
            span = slice(q * length, (q + 1) * length)
            out_gate = part[slot, 1, span, :].astype(jnp.float32)
            mixed[q, 0:8, :] = edges[q, :, at]
            mixed[q, 8:, :] = part[slot, 0, span, :].astype(jnp.float32) * part[slot, 2, span, :].astype(jnp.float32)
            shifted = [mixed[q, 6 + k : 6 + k + length, :] for k in range(3)]
            conv = sum(taps[k : k + 1, at] * shifted[k] for k in range(3))
            grad = gated_grad[span, :]
            proj_back[span, depth + j * 256 : depth + (j + 1) * 256] = (grad * conv).astype(jnp.bfloat16)
            part[slot, 1, span, :] = (out_gate * conv).astype(jnp.bfloat16)
            grad = grad * out_gate
            conv_grad[q, 0:length, at] = grad
            for k in range(3):
                small_own[0, 1 + k : 2 + k, at] += jnp.sum(grad * shifted[k], 0, keepdims=True)
        for h, copy in enumerate(rows_out(j)):
            block[h * 256 : (h + 1) * 256, :] = dot_tn(part[slot, 1], out_back[:, h * chunk : (h + 1) * chunk]).astype(jnp.bfloat16)
            copy.start()

    last = here.s == 3

    def edge_step():
        for copy in rows_out(blocks - 1):
            copy.wait()

        @pl.when(last)
        def _():
            conv_grad[:, length : length + 8, :] = jnp.zeros((seqs, 8, depth), jnp.float32)

        @pl.when(here.s > 0)
        def _():
            remote(conv_grad.at[:, 0:8], conv_grad.at[:, length : length + 8], edge_s, edge_r, (jnp.maximum(here.s - 1, 0), here.f)).start()

    def edge_wait():
        copy = remote(conv_grad.at[:, 0:8], conv_grad.at[:, length : length + 8], edge_s, edge_r, (jnp.maximum(here.s - 1, 0), here.f))

        @pl.when(here.s > 0)
        def _():
            copy.wait_send()

        @pl.when(jnp.logical_not(last))
        def _():
            copy.wait_recv()

    def gate_step(j):
        for copy in part_in(j + blocks):
            copy.wait()
        start_block(j + blocks + 1)
        slot, at = j % 2, slice(j * 256, (j + 1) * 256)
        for q in range(seqs):
            span = slice(q * length, (q + 1) * length)
            grad = sum(taps[2 - k : 3 - k, at] * conv_grad[q, k : k + length, at] for k in range(3))
            proj_back[span, at] = (grad * part[slot, 2, span, :].astype(jnp.float32)).astype(jnp.bfloat16)
            proj_back[span, 2 * depth + j * 256 : 2 * depth + (j + 1) * 256] = (grad * part[slot, 0, span, :].astype(jnp.float32)).astype(jnp.bfloat16)

    def several(*steps):
        def run():
            for step in steps:
                step()

        return run

    columns_done = width // chunk
    start_weights = lambda: weight_in(0).start()
    work = [norm_two_step]
    work += [several(*[functools.partial(conv_step, j) for j in (i, i + 1)]) for i in range(0, blocks, 2)]
    work[-1] = several(work[-1], edge_step)
    work += [several(edge_wait, *[functools.partial(gate_step, j) for j in range(blocks // 2)])]
    work += [several(*[functools.partial(gate_step, j) for j in range(blocks // 2, blocks)], start_weights)]
    work += [functools.partial(grad_in_step, j) for j in range(columns_done)]
    work += [several(lambda: block_out(columns_done - 1).wait(), functools.partial(back_step, 0), functools.partial(back_step, 1))]
    work += [several(*[functools.partial(back_step, j) for j in (i, i + 1)]) for i in range(2, blocks, 2)] + [norm_step]
    work += [functools.partial(small_step, j) for j in range(4)]
    hidden_in.start()
    back_in.start()
    start_block(0)
    stages = [(0, "stage0"), (1, "stage1"), (2, "fetch2"), (3, "fetch3"), (4, "fetch4"), (2, "stage2"), (3, "stage3"), (4, "stage4"), (5, "stage5"), (6, "stage6")]
    seen = [sum(p[0] == q[0] for p in plan[:i]) for i, q in enumerate(plan)]
    assert len(work) <= len(plan) + 6
    for step in range(len(plan) + 6):
        for by, name in stages:
            if 0 <= step - by < len(plan):
                red, t = reducers[plan[step - by][0]], seen[step - by]
                if name == "stage1":
                    stage1(red, t)
                else:
                    getattr(red, name)(t)
        if step < len(work):
            work[step]()
        if step < len(plan):
            ahead(reducers[plan[step][0]], seen[step])
    result_out.wait()
    for i, p in enumerate(plan):
        reducers[p[0]].to_core(seen[i]).wait_send()


def mix(grads, normed, down_in, tokens, edges, taps, gain_one, gain_two, w_in, w_out, projected, back, hidden, plan, kinds, cid):
    view = lambda g: (2, 2, 2, 2, 2, g.shape[0] // 32, g.shape[1])
    counts = [sum(p[0] == k for p in plan) for k in range(len(kinds))]
    sds = jax.ShapeDtypeStruct
    rows, depth = normed.shape
    seqs = edges.shape[0]
    outs = [sds((4,) + view(g)[5:], jnp.bfloat16) for g in [*grads, w_out, w_in]]
    outs += [sds((8, depth), jnp.float32), sds((rows, depth), jnp.float32), sds(w_out.shape, jnp.bfloat16), sds(w_in.shape, jnp.bfloat16)]
    land, scratch, sems = [], [], []
    for (height, width), count in zip(kinds, counts):
        land += landing_shapes(count, False, height, width)
        scratch += scratch_shapes(4, False, height, width)
        sems += sem_shapes(count)
    whole = pl.BlockSpec(memory_space=pltpu.VMEM)
    vmem = pltpu.VMEM
    res = pl.pallas_call(
        functools.partial(mix_kernel, plan, kinds),
        out_shape=outs + land,
        in_specs=[ANY] * len(grads) + [whole] * 7 + [ANY] * 5,
        out_specs=[ANY] * (len(grads) + 2) + [whole] + [ANY] * (3 + len(land)),
        scratch_shapes=scratch
        + sems
        + [DMA((len(kinds),)), vmem((4, 8, depth), jnp.float32), vmem((6, 8, depth), jnp.float32), DMA((6,)), DMA((6,))]
        + [vmem((depth, rows), jnp.bfloat16), vmem((depth, 768), jnp.bfloat16), vmem((2, 256, w_in.shape[1]), jnp.bfloat16)]
        + [vmem((rows, depth), jnp.float32)] * 2
        + [DMA((14,)), vmem((rows, 3 * depth), jnp.bfloat16), vmem((rows, depth), jnp.bfloat16), vmem((seqs, rows // seqs + 8, depth), jnp.float32)]
        + [vmem((2, 3, rows, 256), jnp.bfloat16), vmem((seqs, rows // seqs + 8, 256), jnp.float32)]
        + [DMA, DMA],
        compiler_params=pltpu.CompilerParams(collective_id=cid, has_side_effects=True, vmem_limit_bytes=62 << 20),
        name="mix",
    )(*[g.reshape(view(g)) for g in grads], normed, down_in, tokens, edges, taps, gain_one, gain_two, w_in, w_out, projected, back, hidden)
    return res[: len(grads) + 4]


def from_behind(shard, axis, by):
    count = lax.axis_size(axis)
    pairs = [(i, i + by) for i in range(count) if 0 <= i + by < count]
    return lax.ppermute(shard, axis, pairs)


def norm_rows(token_rows, gain):
    scale = lax.rsqrt(jnp.mean(token_rows * token_rows, -1, keepdims=True) + EPS)
    unit = token_rows * scale
    return (scale, unit, (unit * gain).astype(jnp.bfloat16))


def norm_back(grad, scale, unit, gain):
    gain_grad = jnp.sum(grad * unit, 0)
    inner = grad * gain
    return (gain_grad, scale * (inner - unit * jnp.mean(inner * unit, -1, keepdims=True)))


def left_cross(left, right):
    return lax.dot_general(left, right, (((0,), (0,)), ((), ())), preferred_element_type=jnp.float32)


def against(left, weight):
    return lax.dot_general(left, weight, (((1,), (1,)), ((), ())), preferred_element_type=jnp.float32)


def product(left, right):
    return jnp.dot(left, right, preferred_element_type=jnp.float32)


def routed():
    return lax.axis_size("seq") == 4 and lax.axis_size("fsdp") == 8


def gather_all(shards, axis=0):
    return [lax.all_gather(a, "fsdp", axis=axis, tiled=True) for a in shards]


def reduce_all(grads):
    outs = []
    for g in grads:
        part = lax.psum_scatter(g.astype(jnp.bfloat16), "fsdp", scatter_dimension=0, tiled=True)
        outs.append(lax.psum(part, "seq").astype(jnp.float32))
    return outs


def plan_of(grads):
    kinds = [(48, 768), (216, 256)]
    plan = []
    for i, g in enumerate(grads):
        kind = 0 if g.shape[0] == 1536 else 1
        plan += [(kind, i, column) for column in range(0, g.shape[1], kinds[kind][1])]
    return plan, kinds


def plain(tokens, keep_mask, upstream, down_in, gain_one, conv_taps, gain_two, w_in, w_out, w_gate, w_up, w_down):
    count, block_rows, model_width = tokens.shape
    rows = count * block_rows

    def shifted(value, edge, side):
        value = value.reshape(count, block_rows, model_width)
        return jnp.concatenate([edge, value] if side < 0 else [value, edge], 1)

    def window(value, start):
        return value[:, start : start + block_rows].reshape(rows, model_width)

    token_rows = tokens.reshape(rows, model_width).astype(jnp.float32)
    scale_one, unit_one, normed_one = norm_rows(token_rows, gain_one)
    projected = product(normed_one, w_in)
    in_gate = projected[:, :model_width]
    out_gate = projected[:, model_width : 2 * model_width]
    values = projected[:, 2 * model_width :]
    mixed = in_gate * values
    edge_rows = from_behind(mixed.reshape(count, block_rows, model_width)[:, block_rows - 2 :], "seq", 1)
    extended = shifted(mixed, edge_rows, -1)
    conv_out = conv_taps[0] * window(extended, 0) + conv_taps[1] * window(extended, 1) + conv_taps[2] * window(extended, 2)
    gated = (out_gate * conv_out).astype(jnp.bfloat16)
    hidden_one = token_rows + product(gated, w_out)
    scale_two, unit_two, normed_two = norm_rows(hidden_one, gain_two)
    gate_pre = product(normed_two, w_gate)
    up_pre = product(normed_two, w_up)
    sigmoid_gate = jax.nn.sigmoid(gate_pre)
    silu_value = gate_pre * sigmoid_gate
    activated = (silu_value * up_pre).astype(jnp.bfloat16)
    hidden_two = hidden_one + product(activated, w_down)
    output = (keep_mask * hidden_two).astype(jnp.bfloat16)
    grad_down = left_cross(activated, down_in)
    grad_act = against(down_in, w_down)
    gate_back = (grad_act * up_pre * sigmoid_gate * (1.0 + gate_pre * (1.0 - sigmoid_gate))).astype(jnp.bfloat16)
    up_back = (grad_act * silu_value).astype(jnp.bfloat16)
    grad_gate = left_cross(normed_two, gate_back)
    grad_up = left_cross(normed_two, up_back)
    grad_normed_two = against(gate_back, w_gate) + against(up_back, w_up)
    grad_gain_two, through_two = norm_back(grad_normed_two, scale_two, unit_two, gain_two)
    grad_hidden = upstream + through_two
    out_back = grad_hidden.astype(jnp.bfloat16)
    grad_out = left_cross(gated, out_back)
    grad_gated = against(out_back, w_out)
    grad_out_gate = grad_gated * conv_out
    grad_conv = grad_gated * out_gate
    edge_grad = from_behind(grad_conv.reshape(count, block_rows, model_width)[:, :2], "seq", -1)
    grad_ext = shifted(grad_conv, edge_grad, 1)
    grad_mixed = conv_taps[2] * window(grad_ext, 0) + conv_taps[1] * window(grad_ext, 1) + conv_taps[0] * window(grad_ext, 2)
    grad_taps = [jnp.sum(grad_conv * window(extended, offset), 0) for offset in range(3)]
    proj_back = jnp.concatenate([grad_mixed * values, grad_out_gate, grad_mixed * in_gate], 1).astype(jnp.bfloat16)
    grad_in = left_cross(normed_one, proj_back)
    grad_normed_one = against(proj_back, w_in)
    grad_gain_one, through_one = norm_back(grad_normed_one, scale_one, unit_one, gain_one)
    tokens_grad = grad_hidden + through_one
    small_grads = jnp.stack([grad_gain_one, *grad_taps, grad_gain_two])
    return output, tokens_grad, small_grads, grad_in, grad_out, grad_gate, grad_up, grad_down


def local(tokens, lengths, norm_gain, in_weight, conv_weight, out_weight, ffn_gain, gate_weight, up_weight, down_weight, cotangent):
    count, block_rows, model_width = tokens.shape
    rows = count * block_rows
    width = norm_gain.shape[0]
    rank = lax.axis_index("fsdp")
    small = jnp.concatenate([norm_gain[None], conv_weight, ffn_gain[None]], 0).astype(jnp.float32)
    window = lambda size, start: lax.dynamic_update_slice(jnp.zeros((8, size), jnp.float32), small, (0, start))
    places = lax.axis_index("seq") * block_rows + jnp.arange(block_rows, dtype=jnp.int32)
    keep_mask = (places[None, :] < lengths[:, None]).astype(jnp.float32).reshape(rows, 1)
    upstream = cotangent.reshape(rows, model_width).astype(jnp.float32) * keep_mask
    down_in = upstream.astype(jnp.bfloat16)
    if routed():
        shards = [out_weight, in_weight, gate_weight, up_weight, down_weight]
        token_rows = tokens.reshape(rows, model_width)
        w_out, w_in, w_gate, w_up, w_down, normed_one, projected, edges, vectors, hidden_one, normed_two, mine_t, mate_t = front(shards, window(256, rank * width % 128), token_rows, 0)
        output, grad_normed_two, grad_down, ffn_sums = ffn(normed_two, mine_t, mate_t, down_in, keep_mask, w_gate, w_up, w_down, hidden_one, 1)
        grad_down, grad_out, grad_in, small_grads, tokens_grad = mix(
            [grad_down], normed_one, down_in, token_rows, edges, vectors[1:4], vectors[0:1], vectors[4:5],
            w_in, w_out, projected, grad_normed_two, hidden_one, *plan_of([grad_down, w_out, w_in]), 2,
        )[:5]
        shards = [grad_down, grad_out, grad_in, ffn_sums[0], ffn_sums[1]]
        grad_down, grad_out, grad_in, grad_gate, grad_up = [g.reshape(-1, g.shape[-1]).astype(jnp.float32) for g in shards]
    else:
        w_in, w_out, w_gate, w_up, w_down = gather_all([in_weight, out_weight, gate_weight, up_weight, down_weight])
        vectors = lax.psum(window(model_width, rank * width), "fsdp")
        output, tokens_grad, small_grads, *grads = plain(
            tokens, keep_mask, upstream, down_in, vectors[0], vectors[1:4], vectors[4], w_in, w_out, w_gate, w_up, w_down
        )
        grad_in, grad_out, grad_gate, grad_up, grad_down = reduce_all(grads)
        small_grads = lax.psum(small_grads, ("seq", "fsdp"))
    small_grads = lax.dynamic_slice_in_dim(small_grads, lax.axis_index("fsdp") * width, width, 1)
    return (
        output.reshape(tokens.shape),
        tokens_grad.reshape(tokens.shape),
        small_grads[0],
        grad_in,
        small_grads[1:4],
        grad_out,
        small_grads[4],
        grad_gate,
        grad_up,
        grad_down,
    )


def solution(mesh):
    split = P("fsdp", "seq", None)
    rows, columns, vector = P("fsdp", None), P(None, "fsdp"), P("fsdp")
    return jax.shard_map(
        local,
        mesh=mesh,
        in_specs=(split, vector, vector, rows, columns, rows, vector, rows, rows, rows, split),
        out_specs=(split, split, vector, rows, columns, rows, vector, rows, rows, rows),
        check_vma=False,
    )
```
